256 devices in a mesh: mem: 32 (over z_lo, y, core), lon: 8 (over z_hi, x).
Axes of the slice: x: 4, y: 4, z: 8 (z_hi: 2, z_lo: 4; z = z_hi * 4 + z_lo), core: 2. Of those that a mesh axis runs over, the one named last changes fastest.
Arguments:
- ensemble: bfloat16 [64, 2, 256, 1024], P('mem', None, None, 'lon'), may hold values from -6 to 6
- controls_start: float32 [64, 2, 256, 1024], P('mem', None, None, 'lon'), may hold values from -6 to 6
- kappa_east: float32 [2, 256, 1024], P(None, None, 'lon'), may hold values from 0.02 to 0.24
- kappa_north: float32 [2, 256, 1024], P(None, None, 'lon'), may hold values from 0.02 to 0.24
- innovation: float32 [2, 256, 1024], P(None, 'mem', 'lon'), may hold values from -6 to 6
- obs_mask: int32 [2, 256, 1024], P(None, 'mem', 'lon'), may hold values 0 or 1
- gauge_index: int32 [2, 256, 1024], P(None, 'mem', 'lon'), may hold values from 0 to 63
- gauge_precision: float32 [64], replicated, may hold values from 0.25 to 4
Outputs:
- controls: float32 [64, 2, 256, 1024], P('mem', None, None, 'lon')
- increment: float32 [2, 256, 1024], P(None, 'mem', 'lon')
The draws below stay inside these ranges and needn't reach their ends.
All inputs are finite; a program needn't handle non-finite values. No bound on the sum of `obs_mask` on one device may be relied on, other than what follows from the above.
Results may differ from the reference program's by a relative error of at most 0.0003.
Values sent between devices are 32-bit elements; how exact they have to be, the bound alone decides.
No kernel may reach another device: no remote copies, remote signals or barrier semaphores. Data moves between devices by JAX's collectives and lax.ppermute only.
A program may use at most 64 MiB of HBM per device.

```python
import math
import jax
import jax.numpy as jnp
from jax import lax

LEVELS = 2
LAT = 256
STEPS = 6
ITERS = 2
GAUGES = 64
MEMBERS = 64
LON = 1024


def plant(values, rng, smallest, high):
    longest = values.shape.index(max(values.shape))
    spots = []
    for shift in (0, 1):
        where = [jax.random.randint(jax.random.fold_in(rng, axis), (), 0, length) for axis, length in enumerate(values.shape)]
        where[longest] = (where[longest] + shift) % values.shape[longest]
        spots.append(tuple(where))
    return values.at[spots[0]].set(smallest).at[spots[1]].set(high)


def level_of(own_key, dims, cuts, low, top_value):
    factor_of = 1.0
    for position, blocks in cuts:
        heights = jax.random.uniform(jax.random.fold_in(jax.random.fold_in(own_key, 6), position), (blocks,), jnp.float32, low / len(cuts), top_value / len(cuts))
        factor_of = factor_of * jnp.repeat(jnp.exp(heights), dims[position] // blocks).reshape((-1,) + (1,) * (len(dims) - 1 - position))
    return factor_of


def scatter_about(key, dims, scale, most, pieces=(), held_as=jnp.bfloat16):
    values = jax.random.normal(key, dims, jnp.float32) * scale
    if len(pieces) > 0:
        values = level_of(key, dims, pieces, -0.22, 0.18) * values
    return jnp.clip(values, min=-most, max=most).astype(held_as)


def setup_inputs(seed: int = 0) -> dict:
    streams_of = jax.random.split(jax.random.key(seed), 9)
    ensemble = scatter_about(streams_of[0], (MEMBERS, LEVELS, LAT, LON), 1.0, 6.0, ((0, 32), (3, 8)))
    controls_start = scatter_about(streams_of[1], (MEMBERS, LEVELS, LAT, LON), 1.0, 6.0, ((0, 32), (3, 8)), jnp.float32)
    kappa_east = jnp.clip(0.02 + 0.22 * jax.random.uniform(streams_of[2], (LEVELS, LAT, LON), jnp.float32) ** level_of(streams_of[2], (LEVELS, LAT, LON), ((2, 8),), -0.2, 0.2), 0.02, 0.24)
    kappa_north = jnp.clip(0.02 + 0.22 * jax.random.uniform(streams_of[3], (LEVELS, LAT, LON), jnp.float32) ** level_of(streams_of[3], (LEVELS, LAT, LON), ((2, 8),), -0.2, 0.2), 0.02, 0.24)
    innovation = scatter_about(streams_of[4], (LEVELS, LAT, LON), 1.0, 6.0, ((1, 32), (2, 8)), jnp.float32)
    obs_mask = plant((jax.random.randint(streams_of[5], (LEVELS, LAT, LON), 0, 2) < 1).astype(jnp.int32), jax.random.fold_in(streams_of[5], 1), 0, 1)
    gauge_index = plant(jax.random.randint(streams_of[6], (LEVELS, LAT, LON), 0, GAUGES), jax.random.fold_in(streams_of[6], 1), 0, GAUGES - 1).astype(jnp.int32)
    gauge_precision = jnp.clip(jnp.exp(jax.random.uniform(streams_of[7], (GAUGES,), jnp.float32, math.log(0.25), math.log(4.0))), 0.25, 4.0)
    return {"ensemble": ensemble, "controls_start": controls_start, "kappa_east": kappa_east, "kappa_north": kappa_north, "innovation": innovation, "obs_mask": obs_mask, "gauge_index": gauge_index, "gauge_precision": gauge_precision}


step_size = 0.5


def advance(values, kappa_east, kappa_north):
    east_flux = kappa_east * (jnp.roll(values, -1, axis=-1) - values)
    north_flux = kappa_north[..., :-1, :] * (values[..., 1:, :] - values[..., :-1, :])
    zero_row = jnp.zeros_like(values[..., :1, :])
    upper = jnp.concatenate([north_flux, zero_row], axis=-2)
    lower = jnp.concatenate([zero_row, north_flux], axis=-2)
    return values + east_flux - jnp.roll(east_flux, 1, axis=-1) + upper - lower


def diffuse(values, kappa_east, kappa_north):
    for section in range(STEPS):
        values = advance(values, kappa_east, kappa_north)
    return values


def reference(ensemble, controls_start, kappa_east, kappa_north, innovation, obs_mask, gauge_index, gauge_precision):
    inv_root = float(MEMBERS) ** -0.5
    weight = gauge_precision[gauge_index] * obs_mask.astype(jnp.float32)
    controls = controls_start
    increment = jnp.zeros_like(innovation)
    for iteration in range(ITERS):
        def add_member(total, member_pair):
            member, control = member_pair
            return total + member.astype(jnp.float32) * diffuse(control, kappa_east, kappa_north), None

        total, unused = lax.scan(add_member, jnp.zeros_like(innovation), (ensemble, controls))
        increment = inv_root * total
        forcing = weight * (increment - innovation)

        def adjoint(member):
            return diffuse(inv_root * member.astype(jnp.float32) * forcing, kappa_east, kappa_north)

        gradient = lax.map(adjoint, ensemble)
        controls = controls - step_size * (controls + gradient)
    return controls, increment
```

```python
import jax
import jax.numpy as jnp
from jax import lax
from jax.experimental import pallas as pl
from jax.experimental.pallas import tpu as pltpu
from jax.sharding import PartitionSpec as P

STEPS = 6
GAUGES = 64
step_size = 0.5

BAND = 128
OFF = 32
COLS = BAND + 2 * OFF
REACH = 3 * STEPS
HALO = 4 * STEPS
UNIT = 8
SENT = 2 * HALO + REACH + 2


def tiles(start, count):
    if isinstance(start, int):
        return pl.ds(8 * start, 8 * count)
    return pl.ds(pl.multiple_of(8 * start, 8), 8 * count)


def get(ref, start, count):
    return ref[tiles(start, count), :].reshape(count, 8, 128)


def put(ref, start, value):
    ref[tiles(start, value.shape[0]), :] = value.reshape(-1, 128)


def sublane():
    return lax.broadcasted_iota(jnp.int32, (1, 8, 128), 1)


def lane():
    return lax.broadcasted_iota(jnp.int32, (1, 8, 128), 2)


def for_blocks(lo, hi, work):
    count = -(-(hi - lo) // UNIT)

    def step(block, carry):
        work(lo + UNIT * block)
        return carry

    lax.fori_loop(0, count, step, 0)


def diffuse(source, spare, same, other, east, lo, hi):
    upper = sublane() >= 4
    for section in range(STEPS):
        lo, hi = lo + 1, hi - 1
        src, dst = (source, spare) if section % 2 == 0 else (spare, source)

        def work(at, src=src, dst=dst):
            values = get(src, at - 1, UNIT + 2)
            flux = get(east, at - 1, UNIT + 1) * (values[1:] - values[:-1])
            inner = values[1:-1]
            pair = pltpu.roll(inner, 4, 1)
            next_pair = jnp.where(upper, pltpu.roll(pair, 127, 2), pltpu.roll(pair, 1, 2))
            change = get(same, at, UNIT) * (pair - inner) + get(other, at, UNIT) * (next_pair - inner)
            put(dst, at, inner + (flux[1:] - flux[:-1]) + change)

        for_blocks(lo, hi, work)


def prepare_kernel(controls, ensemble, kappa_east, kappa_north, innovation, mask, gauge, precision,
                   c_out, k_out, e_out, w_out, right, left, wide):
    for member in range(2):
        for level in range(2):
            for parity in range(2):
                row = 4 * parity + 2 * member + level
                part = controls[member, level, pl.ds(parity, 128, stride=2), :]
                c_out[pl.ds(row, 128, stride=8), :] = part.T
                if parity == 0:
                    wide[...] = ensemble[member, level].astype(jnp.float32)
                e_out[pl.ds(row, 128, stride=8), :] = wide[pl.ds(parity, 128, stride=2), :].T
    for kind, kappa in enumerate((kappa_east, kappa_north)):
        for level in range(2):
            for parity in range(2):
                row = 4 * parity + 2 * kind + level
                k_out[pl.ds(row, 128, stride=8), :] = kappa[level, pl.ds(parity, 128, stride=2), :].T
    at = 0
    for part, width in ((c_out, HALO), (k_out, HALO), (e_out, REACH)):
        put(right, at, get(part, BAND - width, width))
        put(left, at, get(part, 0, width))
        at += width
    index = gauge[...]
    found = jnp.zeros(index.shape, jnp.float32)
    for label in range(GAUGES):
        found = jnp.where(index == label, precision[0, label], found)
    weight = found * mask[...].astype(jnp.float32)
    w_out[...] = weight
    lanes = lax.broadcasted_iota(jnp.int32, (8, 128), 1)
    for value in (weight, innovation[...]):
        to_right = jnp.zeros((8, 128), jnp.float32)
        to_left = jnp.zeros((8, 128), jnp.float32)
        for level in range(2):
            spot = 64 * level
            moved = pltpu.roll(value[level], (spot + REACH) % 128, 1)
            to_right = jnp.where((lanes >= spot) & (lanes < spot + REACH), moved, to_right)
            spot = 64 * level + 32
            moved = pltpu.roll(value[level], spot, 1)
            to_left = jnp.where((lanes >= spot) & (lanes < spot + REACH), moved, to_left)
        put(right, at, to_right[None])
        put(left, at, to_left[None])
        at += 1


def extend(band, from_left, from_right, out, at, width):
    put(out, OFF - width, get(from_left, at, width))
    put(out, OFF + BAND, get(from_right, at, width))
    out[tiles(OFF, BAND), :] = band[...]


def sum_members(values, ensemble, product, plain, out, blocks):
    def work(at):
        term = get(ensemble, at, UNIT) * get(values, at, UNIT)
        put(product, at, term + pltpu.roll(term, 6, 1))

    for_blocks(OFF - 24, OFF + BAND + 24, work)
    for parity in range(2):
        edges = []
        for level in range(2):
            row = 4 * parity + level
            part = product[pl.ds(8 * OFF + row, 128, stride=8), :]
            plain[level, pl.ds(parity, 128, stride=2), :] = part.T
            edges.append(product[pl.ds(8 * (OFF - REACH) + row, 32, stride=8), :])
            edges.append(product[pl.ds(8 * (OFF + BAND) + row, 32, stride=8), :])
        plain[2, pl.ds(parity, 128, stride=2), :] = jnp.concatenate(edges, axis=0).T
    for tile in range(3):
        out[:, tile] = plain[tile].reshape(blocks, 8, 128)


def spread(parts, plain, forcing):
    for tile in range(3):
        plain[tile] = parts[:, tile].reshape(256, 128)
    for parity in range(2):
        edges = plain[2, pl.ds(parity, 128, stride=2), :].T
        for level in range(2):
            band = plain[level, pl.ds(parity, 128, stride=2), :].T
            for member in range(2):
                row = 4 * parity + 2 * member + level
                left = edges[64 * level : 64 * level + 24]
                right = edges[64 * level + 32 : 64 * level + 56]
                forcing[pl.ds(8 * (OFF - REACH) + row, 24, stride=8), :] = left
                forcing[pl.ds(8 * (OFF + BAND) + row, 24, stride=8), :] = right
                forcing[pl.ds(8 * OFF + row, 128, stride=8), :] = band


def first_kernel(c_in, k_in, e_in, w_in, innovation, from_left, from_right,
                 out, c_out, e_out, same, other, east, w_out, i_out, values, spare, plain):
    blocks = out.shape[0]
    extend(c_in, from_left, from_right, c_out, 0, HALO)
    extend(k_in, from_left, from_right, spare, HALO, HALO)
    extend(e_in, from_left, from_right, e_out, 2 * HALO, REACH)
    upper = sublane() >= 4
    second = sublane() % 4 >= 2
    edge = (upper & (lane() == 127)) | (~upper & (lane() == 0))

    def coefs(at):
        both = get(spare, at, UNIT)
        put(east, at, jnp.where(second, pltpu.roll(both, 2, 1), both))
        north = jnp.where(second, both, pltpu.roll(both, 6, 1))
        swapped = pltpu.roll(north, 4, 1)
        put(same, at, jnp.where(upper, swapped, north))
        put(other, at, jnp.where(edge, 0.0, jnp.where(upper, north, pltpu.roll(swapped, 1, 2))))
        put(values, at, get(c_out, at, UNIT))

    for_blocks(OFF - HALO, OFF + BAND + HALO, coefs)
    for row, (band, result) in enumerate(((w_in, w_out), (innovation, i_out))):
        at = 2 * HALO + REACH + row
        result[:2] = band[...]
        result[2:] = get(from_left, at, 1) + get(from_right, at, 1)
    diffuse(values, spare, same, other, east, OFF - HALO, OFF + BAND + HALO)
    sum_members(values, e_out, spare, plain, out, blocks)


def forcing_kernel(parts, weight, innovation, out, increment, *, scale):
    total = parts[0]
    for block in range(1, parts.shape[0]):
        total = total + parts[block]
    total = scale * total
    increment[...] = total[:2]
    forcing = weight[...] * (total - innovation[...])
    for block in range(out.shape[0]):
        out[block] = forcing


def middle_kernel(parts, c_in, e_in, same, other, east, out, c_out, values, spare, plain, *, scale):
    blocks = out.shape[0]
    spread(parts, plain, values)

    def start(at):
        put(values, at, scale * get(e_in, at, UNIT) * get(values, at, UNIT))

    for_blocks(OFF - REACH, OFF + BAND + REACH, start)
    diffuse(values, spare, same, other, east, OFF - REACH, OFF + BAND + REACH)

    def update(at):
        new = get(c_in, at, UNIT)
        new = new - step_size * (new + get(values, at, UNIT))
        put(c_out, at, new)
        put(values, at, new)

    for_blocks(OFF - 2 * STEPS, OFF + BAND + 2 * STEPS, update)
    diffuse(values, spare, same, other, east, OFF - 2 * STEPS, OFF + BAND + 2 * STEPS)
    sum_members(values, e_in, spare, plain, out, blocks)


def last_kernel(parts, c_in, e_in, same, other, east, out, values, spare, plain, *, scale):
    spread(parts, plain, values)

    def start(at):
        put(values, at, scale * get(e_in, at, UNIT) * get(values, at, UNIT))

    for_blocks(OFF - STEPS, OFF + BAND + STEPS, start)
    diffuse(values, spare, same, other, east, OFF - STEPS, OFF + BAND + STEPS)

    def update(at):
        new = get(c_in, at, UNIT)
        put(values, at, new - step_size * (new + get(values, at, UNIT)))

    for_blocks(OFF, OFF + BAND, update)
    for member in range(2):
        for level in range(2):
            for parity in range(2):
                row = 4 * parity + 2 * member + level
                part = values[pl.ds(8 * OFF + row, 128, stride=8), :]
                out[member, level, pl.ds(parity, 128, stride=2), :] = part.T


def call(kernel, outs, scratch, name, *args):
    return pl.pallas_call(
        kernel,
        out_shape=[jax.ShapeDtypeStruct(shape, jnp.float32) for shape in outs],
        in_specs=[pl.BlockSpec(memory_space=pltpu.VMEM)] * len(args),
        out_specs=[pl.BlockSpec(memory_space=pltpu.VMEM)] * len(outs),
        scratch_shapes=[pltpu.VMEM(shape, jnp.float32) for shape in scratch],
        name=name,
    )(*args)


def swap(parts):
    return lax.all_to_all(parts, "mem", split_axis=0, concat_axis=0, tiled=True)


def body(ensemble, controls_start, kappa_east, kappa_north, innovation, obs_mask, gauge_index, gauge_precision):
    blocks = lax.axis_size("mem")
    bands = lax.axis_size("lon")
    scale = float(blocks * ensemble.shape[0]) ** (-0.5)
    band, wide, plain = (8 * BAND, 128), (8 * COLS, 128), (3, 256, 128)
    parcel, parts = (8 * SENT, 128), (blocks, 3, 8, 128)
    c, k, e, w, right, left = call(
        prepare_kernel, (band, band, band, innovation.shape, parcel, parcel), ((256, 128),), "prepare",
        controls_start, ensemble, kappa_east, kappa_north, innovation, obs_mask, gauge_index,
        gauge_precision.reshape(1, GAUGES),
    )
    from_left = lax.ppermute(right, "lon", [(i, (i + 1) % bands) for i in range(bands)])
    from_right = lax.ppermute(left, "lon", [((i + 1) % bands, i) for i in range(bands)])
    sums, c, e, same, other, east, weight, innov = call(
        first_kernel, (parts, wide, wide, wide, wide, wide, (3, 8, 128), (3, 8, 128)), (wide, wide, plain), "first",
        c, k, e, w, innovation, from_left, from_right,
    )

    def forced(sums):
        kernel = lambda *refs: forcing_kernel(*refs, scale=scale)
        return call(kernel, (parts, innovation.shape), (), "forcing", swap(sums), weight, innov)

    forcing, _ = forced(sums)
    kernel = lambda *refs: middle_kernel(*refs, scale=scale)
    sums, c = call(kernel, (parts, wide), (wide, wide, plain), "middle", swap(forcing), c, e, same, other, east)
    forcing, increment = forced(sums)
    kernel = lambda *refs: last_kernel(*refs, scale=scale)
    (controls,) = call(
        kernel, (controls_start.shape,), (wide, wide, plain), "last", swap(forcing), c, e, same, other, east
    )
    return controls, increment


def solution(mesh):
    in_specs = (
        P("mem", None, None, "lon"),
        P("mem", None, None, "lon"),
        P(None, None, "lon"),
        P(None, None, "lon"),
        P(None, "mem", "lon"),
        P(None, "mem", "lon"),
        P(None, "mem", "lon"),
        P(),
    )
    out_specs = (P("mem", None, None, "lon"), P(None, "mem", "lon"))
    return jax.shard_map(body, mesh=mesh, in_specs=in_specs, out_specs=out_specs, check_vma=False)
```

```python
import jax
import jax.numpy as jnp
from jax import lax
from jax.experimental import pallas as pl
from jax.experimental.pallas import tpu as pltpu
from jax.sharding import PartitionSpec as P

STEPS = 6
GAUGES = 64
step_size = 0.5

UNROLL = True
BAND = 128
PAD = 8
HALO = 4 * STEPS
REACH = 3 * STEPS
SPAN = HALO + BAND // 2
SIZE = PAD + SPAN + PAD
UNIT = 8
SENT = 2 * HALO + REACH + 2


def tiles(place, count):
    if isinstance(place, int):
        return pl.ds(8 * (PAD + place), 8 * count)
    return pl.ds(pl.multiple_of(8 * (PAD + place), 8), 8 * count)


def get(ref, place, count):
    return ref[tiles(place, count), :].reshape(count, 8, 128)


def put(ref, place, value):
    ref[tiles(place, value.shape[0]), :] = value.reshape(-1, 128)


def rows(place, row, count):
    return pl.ds(8 * (PAD + place) + row, count, stride=8)


def lane_index():
    return lax.broadcasted_iota(jnp.int32, (1, 8, 128), 2)


def row_index():
    return lax.broadcasted_iota(jnp.int32, (1, 8, 128), 1)


def flipped(value):
    groups = value.reshape(-1, 8, 128)
    index = 7 - lax.broadcasted_iota(jnp.int32, groups.shape, 1)
    groups = jnp.take_along_axis(groups, index, axis=1)
    count = groups.shape[0]
    return jnp.concatenate([groups[count - 1 - i] for i in range(count)], axis=0)


def halves_of(band):
    return band[:64], flipped(band[64:])


def band_of(ref, row):
    first = ref[rows(HALO, row, 64), :]
    return jnp.concatenate([first, flipped(ref[rows(HALO, row + 4, 64), :])], axis=0)


def for_blocks(lo, work):
    count = -(-(SPAN - lo) // UNIT)
    first = SPAN - UNIT * count

    def step(block, carry):
        work(first + UNIT * block)
        return carry

    lax.fori_loop(0, count, step, 0)


def join(ref):
    put(ref, SPAN, pltpu.roll(get(ref, SPAN - 1, 1), 4, 1))


def diffuse(source, spare, east, same, other, lo):
    for parity in range(2):
        join(source.at[parity])
    for section in range(STEPS):
        lo += 1
        src, dst = (source, spare) if section % 2 == 0 else (spare, source)
        count = -(-(SPAN - lo) // UNIT)
        first = SPAN - UNIT * count

        def block(at, carry, src=src, dst=dst):
            ahead, *before = carry
            even, odd = (get(src.at[parity], at, UNIT + 1) for parity in range(2))
            across = get(other, at, UNIT) * (ahead - odd[:-1])
            back = pltpu.roll(across, 1, 2)
            next_ahead = pltpu.roll(get(src.at[0], at + UNIT, UNIT), 127, 2)
            within = get(same, at, UNIT) * (odd[:-1] - even[:-1])
            after = []
            for parity, values, north in ((1, odd, across - within), (0, even, None)):
                flux = get(east.at[parity], at, UNIT) * (values[1:] - values[:-1])
                change = flux - jnp.concatenate([before[parity], flux[:-1]], axis=0)
                if north is None:
                    north = within - back
                put(dst.at[parity], at, (values[:-1] + change) + north)
                after.insert(0, flux[-1:])
            return (next_ahead, *after)

        ahead = pltpu.roll(get(src.at[0], first, UNIT), 127, 2)
        before = [
            get(east.at[parity], first - 1, 1)
            * (get(src.at[parity], first, 1) - get(src.at[parity], first - 1, 1))
            for parity in range(2)
        ]
        carry = (ahead, *before)
        if UNROLL:
            for i in range(count):
                carry = block(first + UNIT * i, carry)
        else:
            carry = lax.fori_loop(0, count, lambda i, c, block=block, first=first: block(first + UNIT * i, c), carry)
        for parity in range(2):
            join(dst.at[parity])


def prepare_kernel(controls, ensemble, kappa_east, kappa_north, innovation, mask, gauge, precision,
                   c_out, k_out, e_out, w_out, first, second, wide):
    odd = lax.axis_index("lon") % 2 == 1

    def lay(values, parity, row, out):
        for half, part in enumerate(halves_of(values.T)):
            out[parity, rows(HALO, row + 4 * half, 64), :] = part

    for member in range(2):
        for level in range(2):
            row = 2 * member + level
            wide[...] = ensemble[member, level].astype(jnp.float32)
            for parity in range(2):
                lay(controls[member, level, pl.ds(parity, 128, stride=2), :], parity, row, c_out)
                lay(wide[pl.ds(parity, 128, stride=2), :], parity, row, e_out)
    for kind, kappa in enumerate((kappa_east, kappa_north)):
        for level in range(2):
            for parity in range(2):
                lay(kappa[level, pl.ds(parity, 128, stride=2), :], parity, 2 * kind + level, k_out)
    low = row_index() < 4
    at = 0

    def send(right, left):
        right, left = right.reshape(8, 128), left.reshape(8, 128)
        first[8 * at : 8 * (at + 1), :] = jnp.where(odd, right, left)
        second[8 * at : 8 * (at + 1), :] = jnp.where(odd, left, right)

    for part, width in ((c_out, HALO), (k_out, HALO), (e_out, REACH)):
        for place in range(HALO - width, HALO):
            one, two = (get(part.at[parity], 2 * HALO - 1 - place, 1) for parity in range(2))
            send(jnp.where(low, pltpu.roll(one, 4, 1), two), jnp.where(low, one, pltpu.roll(two, 4, 1)))
            at += 1
    index = gauge[...]
    found = jnp.zeros(index.shape, jnp.float32)
    for label in range(GAUGES):
        found = jnp.where(index == label, precision[0, label], found)
    weight = found * mask[...].astype(jnp.float32)
    w_out[...] = weight
    lanes = lax.broadcasted_iota(jnp.int32, (8, 128), 1)
    for value in (weight, innovation[...]):
        to_right = jnp.zeros((8, 128), jnp.float32)
        to_left = jnp.zeros((8, 128), jnp.float32)
        for level in range(2):
            place = lanes - 64 * level
            moved = jnp.take_along_axis(value[level], jnp.clip(BAND - HALO + place, 0, 127), axis=1)
            to_right = jnp.where((place >= HALO - REACH) & (place < HALO), moved, to_right)
            place = place - 32
            moved = jnp.take_along_axis(value[level], jnp.clip(HALO - 1 - place, 0, 127), axis=1)
            to_left = jnp.where((place >= HALO - REACH) & (place < HALO), moved, to_left)
        send(to_right, to_left)
        at += 1


def received(first, second, at):
    odd = lax.axis_index("lon") % 2 == 1
    one, two = (part[8 * at : 8 * (at + 1), :].reshape(1, 8, 128) for part in (first, second))
    return jnp.where(odd, two, one), jnp.where(odd, one, two)


def extend(band, first, second, out, at, width):
    low = row_index() < 4
    for place in range(HALO - width, HALO):
        one, two = received(first, second, at)
        put(out.at[0], place, jnp.where(low, one, pltpu.roll(two, 4, 1)))
        put(out.at[1], place, jnp.where(low, pltpu.roll(one, 4, 1), two))
        at += 1
    for parity in range(2):
        out[parity, tiles(HALO, SPAN - HALO), :] = band[parity, tiles(HALO, SPAN - HALO), :]


def block_rows(chip, own):
    core = lax.axis_index("mem") % 2
    if not own:
        core = 1 - core
    return pl.ds(pl.multiple_of(16 * chip + 8 * core, 8), 8)


def sum_members(values, ensemble, product, plain, mine, other_core, lo):
    def work(at):
        for parity in range(2):
            term = get(ensemble.at[parity], at, UNIT) * get(values.at[parity], at, UNIT)
            put(product.at[parity], at, term + pltpu.roll(term, 6, 1))

    for_blocks(lo, work)
    for parity in range(2):
        edges = []
        for level in range(2):
            plain[level, pl.ds(parity, 128, stride=2), :] = band_of(product.at[parity], level).T
            for half in range(2):
                edges.append(product[parity, rows(0, level + 4 * half, 32), :])
        plain[2, pl.ds(parity, 128, stride=2), :] = jnp.concatenate(edges, axis=0).T
    for tile in range(3):
        for chip in range(mine.shape[0]):
            mine[chip, tile] = plain[tile, block_rows(chip, True), :]
            other_core[chip, tile] = plain[tile, block_rows(chip, False), :]


def spread(mine, other_core, plain, forcing):
    for tile in range(3):
        for chip in range(mine.shape[0]):
            plain[tile, block_rows(chip, True), :] = mine[chip, tile]
            plain[tile, block_rows(chip, False), :] = other_core[chip, tile]
    for parity in range(2):
        edges = plain[2, pl.ds(parity, 128, stride=2), :].T
        for level in range(2):
            halves = halves_of(plain[level, pl.ds(parity, 128, stride=2), :].T)
            for half in range(2):
                edge = edges[64 * level + 32 * half : 64 * level + 32 * half + HALO]
                for member in range(2):
                    row = 4 * half + 2 * member + level
                    forcing[parity, rows(0, row, HALO), :] = edge
                    forcing[parity, rows(HALO, row, 64), :] = halves[half]


def first_kernel(c_in, k_in, e_in, w_in, innovation, near, far,
                 mine, other_core, c_out, e_out, east, same, other, w_out, i_out, values, spare, plain):
    extend(c_in, near, far, c_out, 0, HALO)
    extend(k_in, near, far, spare, HALO, HALO)
    extend(e_in, near, far, e_out, 2 * HALO, REACH)
    low = row_index() < 4
    second = row_index() % 4 >= 2
    last = lane_index() == 127
    for parity in range(2):
        join(spare.at[parity])

    def coefs(at):
        for parity in range(2):
            both = get(spare.at[parity], at, UNIT + 1)
            face = jnp.where(low, both[:-1], both[1:])
            put(east.at[parity], at, jnp.where(second, pltpu.roll(face, 2, 1), face))
            north = jnp.where(second, both[:-1], pltpu.roll(both[:-1], 6, 1))
            if parity == 0:
                put(same, at, north)
            else:
                put(other, at, jnp.where(last, 0.0, north))
            put(values.at[parity], at, get(c_out.at[parity], at, UNIT))

    for_blocks(0, coefs)
    for row, (band, result) in enumerate(((w_in, w_out), (innovation, i_out))):
        at = 2 * HALO + REACH + row
        result[:2] = band[...]
        result[2] = near[8 * at : 8 * (at + 1), :] + far[8 * at : 8 * (at + 1), :]
    diffuse(values, spare, east, same, other, 0)
    sum_members(values, e_out, spare, plain, mine, other_core, STEPS)


def forcing_kernel(parts, weight, innovation, out, increment, *, scale):
    total = parts[0]
    for block in range(1, parts.shape[0]):
        total = total + parts[block]
    total = scale * total
    increment[...] = total[:2]
    forcing = weight[...] * (total - innovation[...])
    for block in range(out.shape[0]):
        out[block] = forcing


def gradient(e_in, east, same, other, values, spare, scale, lo):
    def start(at):
        for parity in range(2):
            term = get(e_in.at[parity], at, UNIT) * get(values.at[parity], at, UNIT)
            put(values.at[parity], at, scale * term)

    for_blocks(lo, start)
    diffuse(values, spare, east, same, other, lo)


def middle_kernel(mine, other_core, c_in, e_in, east, same, other, mine_out, other_out, c_out, values, spare, plain, *, scale):
    spread(mine, other_core, plain, values)
    gradient(e_in, east, same, other, values, spare, scale, STEPS)

    def update(at):
        for parity in range(2):
            new = get(c_in.at[parity], at, UNIT)
            new = new - step_size * (new + get(values.at[parity], at, UNIT))
            put(c_out.at[parity], at, new)
            put(values.at[parity], at, new)

    for_blocks(2 * STEPS, update)
    diffuse(values, spare, east, same, other, 2 * STEPS)
    sum_members(values, e_in, spare, plain, mine_out, other_out, 3 * STEPS)


def last_kernel(mine, other_core, c_in, e_in, east, same, other, out, values, spare, plain, *, scale):
    spread(mine, other_core, plain, values)
    gradient(e_in, east, same, other, values, spare, scale, 3 * STEPS)

    def update(at):
        for parity in range(2):
            new = get(c_in.at[parity], at, UNIT)
            put(values.at[parity], at, new - step_size * (new + get(values.at[parity], at, UNIT)))

    for_blocks(HALO, update)
    for member in range(2):
        for level in range(2):
            for parity in range(2):
                part = band_of(values.at[parity], 2 * member + level)
                out[member, level, pl.ds(parity, 128, stride=2), :] = part.T


def call(kernel, outs, scratch, name, *args):
    return pl.pallas_call(
        kernel,
        out_shape=[jax.ShapeDtypeStruct(shape, jnp.float32) for shape in outs],
        in_specs=[pl.BlockSpec(memory_space=pltpu.VMEM)] * len(args),
        out_specs=[pl.BlockSpec(memory_space=pltpu.VMEM)] * len(outs),
        scratch_shapes=[pltpu.VMEM(shape, jnp.float32) for shape in scratch],
        name=name,
    )(*args)


def swap_chips(parts):
    size = lax.axis_size("mem")
    groups = [list(range(core, size, 2)) for core in range(2)]
    return lax.all_to_all(parts, "mem", split_axis=0, concat_axis=0, tiled=True, axis_index_groups=groups)


def swap_cores(part):
    return lax.ppermute(part, "mem", [(i, i ^ 1) for i in range(lax.axis_size("mem"))])


def swap_bands(part, odd_up):
    bands = lax.axis_size("lon")
    return lax.ppermute(part, "lon", [(i, (i + 1 if (i % 2 == 1) == odd_up else i - 1) % bands) for i in range(bands)])


def body(ensemble, controls_start, kappa_east, kappa_north, innovation, obs_mask, gauge_index, gauge_precision):
    chips = lax.axis_size("mem") // 2
    scale = float(lax.axis_size("mem") * ensemble.shape[0]) ** (-0.5)
    field, one, plain = (2, 8 * SIZE, 128), (8 * SIZE, 128), (3, 256, 128)
    parcel, parts = (8 * SENT, 128), (chips, 3, 8, 128)
    c, k, e, w, first, second = call(
        prepare_kernel, (field, field, field, innovation.shape, parcel, parcel), ((256, 128),), "prepare",
        controls_start, ensemble, kappa_east, kappa_north, innovation, obs_mask, gauge_index,
        gauge_precision.reshape(1, GAUGES),
    )
    near, far = swap_bands(first, True), swap_bands(second, False)
    mine, theirs, c, e, east, same, other, weight, innov = call(
        first_kernel, (parts, parts, field, field, field, one, one, (3, 8, 128), (3, 8, 128)), (field, field, plain),
        "first", c, k, e, w, innovation, near, far,
    )

    def forced(mine, theirs):
        kernel = lambda *refs: forcing_kernel(*refs, scale=scale)
        sums = swap_chips(mine + swap_cores(theirs))
        forcing, increment = call(kernel, (parts, innovation.shape), (), "forcing", sums, weight, innov)
        mine = swap_chips(forcing)
        return mine, swap_cores(mine), increment

    mine, theirs, _ = forced(mine, theirs)
    kernel = lambda *refs: middle_kernel(*refs, scale=scale)
    mine, theirs, c = call(
        kernel, (parts, parts, field), (field, field, plain), "middle", mine, theirs, c, e, east, same, other
    )
    mine, theirs, increment = forced(mine, theirs)
    kernel = lambda *refs: last_kernel(*refs, scale=scale)
    (controls,) = call(
        kernel, (controls_start.shape,), (field, field, plain), "last", mine, theirs, c, e, east, same, other
    )
    return controls, increment


def solution(mesh):
    in_specs = (
        P("mem", None, None, "lon"),
        P("mem", None, None, "lon"),
        P(None, None, "lon"),
        P(None, None, "lon"),
        P(None, "mem", "lon"),
        P(None, "mem", "lon"),
        P(None, "mem", "lon"),
        P(),
    )
    out_specs = (P("mem", None, None, "lon"), P(None, "mem", "lon"))
    return jax.shard_map(body, mesh=mesh, in_specs=in_specs, out_specs=out_specs, check_vma=False)
```

```python
import jax
import jax.numpy as jnp
from jax import lax
from jax.experimental import pallas as pl
from jax.experimental.pallas import tpu as pltpu
from jax.sharding import PartitionSpec as P

STEPS = 6
GAUGES = 64
step_size = 0.5

BAND = 128
PAD = 1
HALO = 4 * STEPS
REACH = 3 * STEPS
SPAN = HALO + BAND // 2
SIZE = PAD + SPAN + PAD
UNIT = 8
SENT = 2 * HALO + REACH + 2


def tiles(place, count):
    if isinstance(place, int):
        return pl.ds(8 * (PAD + place), 8 * count)
    return pl.ds(pl.multiple_of(8 * (PAD + place), 8), 8 * count)


def get(ref, place, count):
    return ref[tiles(place, count), :].reshape(count, 8, 128)


def put(ref, place, value):
    ref[tiles(place, value.shape[0]), :] = value.reshape(-1, 128)


def rows(place, row, count):
    return pl.ds(8 * (PAD + place) + row, count, stride=8)


def lane_index():
    return lax.broadcasted_iota(jnp.int32, (1, 8, 128), 2)


def row_index():
    return lax.broadcasted_iota(jnp.int32, (1, 8, 128), 1)


def flipped(value):
    groups = value.reshape(-1, 8, 128)
    index = 7 - lax.broadcasted_iota(jnp.int32, groups.shape, 1)
    groups = jnp.take_along_axis(groups, index, axis=1)
    count = groups.shape[0]
    return jnp.concatenate([groups[count - 1 - i] for i in range(count)], axis=0)


def halves_of(band):
    return band[:64], flipped(band[64:])


def band_of(ref, row):
    first = ref[rows(HALO, row, 64), :]
    return jnp.concatenate([first, flipped(ref[rows(HALO, row + 4, 64), :])], axis=0)


def blocks_from(lo, hi=SPAN):
    return range(hi - UNIT * -(-(hi - lo) // UNIT), hi, UNIT)


def join(ref):
    put(ref, SPAN, pltpu.roll(get(ref, SPAN - 1, 1), 4, 1))


def diffuse(source, spare, east, same, other, spans, joined=True, before_step=None):
    def opening(src, first):
        before = []
        for parity in range(2):
            pair = get(src.at[parity], first - 1, 2)
            before.append(get(east.at[parity], first - 1, 1) * (pair[1:] - pair[:1]))
        return pltpu.roll(get(src.at[0], first, UNIT), 127, 2), *before

    if joined:
        for parity in range(2):
            join(source.at[parity])
    carry = opening(source, spans[0][0])
    for section, (first, end) in enumerate(spans):
        src, dst = (source, spare) if section % 2 == 0 else (spare, source)
        if before_step is not None:
            before_step(section, src)
        ahead, *before = carry
        for at in range(first, end, UNIT):
            even, odd = (get(src.at[parity], at, UNIT + 1) for parity in range(2))
            across = get(other, at, UNIT) * (ahead - odd[:-1])
            back = pltpu.roll(across, 1, 2)
            if at + UNIT < end:
                ahead = pltpu.roll(get(src.at[0], at + UNIT, UNIT), 127, 2)
            elif section + 1 < STEPS:
                carry = opening(dst, spans[section + 1][0])
            within = get(same, at, UNIT) * (odd[:-1] - even[:-1])
            for parity, values in ((1, odd), (0, even)):
                flux = get(east.at[parity], at, UNIT) * (values[1:] - values[:-1])
                change = flux - jnp.concatenate([before[parity], flux[:-1]], axis=0)
                north = across - within if parity else within - back
                put(dst.at[parity], at, (values[:-1] + change) + north)
                before[parity] = flux[-1:]
        if joined:
            for parity in range(2):
                join(dst.at[parity])


def inward(lo):
    return [(blocks_from(lo + step)[0], SPAN) for step in range(1, STEPS + 1)]


def edges_kernel(controls, ensemble, kappa_east, kappa_north, innovation, mask, gauge, precision,
                 w_out, i_out, first, second, right, left, wide):
    odd = lax.axis_index("lon") % 2 == 1

    def send(values, at, row):
        turned = values.T
        right[pl.ds(8 * at + row, HALO, stride=8), :] = turned[BAND - HALO :]
        left[pl.ds(8 * at + row, HALO, stride=8), :] = flipped(turned[:HALO])

    for member in range(2):
        for level in range(2):
            row = 2 * member + level
            wide[...] = ensemble[member, level].astype(jnp.float32)
            for parity in range(2):
                send(controls[member, level, pl.ds(parity, 128, stride=2), :], 0, 4 * parity + row)
                send(wide[pl.ds(parity, 128, stride=2), :], HALO + REACH, 4 * parity + row)
    for kind, kappa in enumerate((kappa_east, kappa_north)):
        for level in range(2):
            for parity in range(2):
                send(kappa[level, pl.ds(parity, 128, stride=2), :], HALO, 4 * parity + 2 * kind + level)
    index = gauge[...]
    found = jnp.zeros(index.shape, jnp.float32)
    for label in range(GAUGES):
        found = jnp.where(index == label, precision[0, label], found)
    weight = found * mask[...].astype(jnp.float32)
    w_out[...] = weight
    i_out[...] = innovation[...]
    lanes = lax.broadcasted_iota(jnp.int32, (8, 128), 1)
    at = 2 * HALO + REACH
    for value in (weight, innovation[...]):
        to_right = jnp.zeros((8, 128), jnp.float32)
        to_left = jnp.zeros((8, 128), jnp.float32)
        for level in range(2):
            place = lanes - 64 * level
            moved = jnp.take_along_axis(value[level], jnp.clip(BAND - HALO + place, 0, 127), axis=1)
            to_right = jnp.where((place >= HALO - REACH) & (place < HALO), moved, to_right)
            place = place - 32
            moved = jnp.take_along_axis(value[level], jnp.clip(HALO - 1 - place, 0, 127), axis=1)
            to_left = jnp.where((place >= HALO - REACH) & (place < HALO), moved, to_left)
        right[8 * at : 8 * (at + 1), :] = to_right
        left[8 * at : 8 * (at + 1), :] = to_left
        at += 1
    first[...] = jnp.where(odd, right[...], left[...])
    second[...] = jnp.where(odd, left[...], right[...])


def coefficients(raw, east, same, other, blocks):
    low = row_index() < 4
    second = row_index() % 4 >= 2
    last = lane_index() == 127
    for at in blocks:
        for parity in range(2):
            both = get(raw.at[parity], at, UNIT + 1)
            face = jnp.where(low, both[:-1], both[1:])
            put(east.at[parity], at, jnp.where(second, pltpu.roll(face, 2, 1), face))
            north = jnp.where(second, both[:-1], pltpu.roll(both[:-1], 6, 1))
            if parity == 0:
                put(same, at, north)
            else:
                put(other, at, jnp.where(last, 0.0, north))


def multiply(values, ensemble, product, blocks):
    for at in blocks:
        for parity in range(2):
            term = get(ensemble.at[parity], at, UNIT) * get(values.at[parity], at, UNIT)
            put(product.at[parity], at, term + pltpu.roll(term, 6, 1))


def inner_kernel(controls, ensemble, kappa_east, kappa_north,
                 c_out, e_out, east, same, other, product, saved, values, spare, raw, wide):
    def lay(values, parity, row, *outs):
        for half, part in enumerate(halves_of(values.T)):
            for out in outs:
                out[parity, rows(HALO, row + 4 * half, 64), :] = part

    for member in range(2):
        for level in range(2):
            row = 2 * member + level
            wide[...] = ensemble[member, level].astype(jnp.float32)
            for parity in range(2):
                lay(controls[member, level, pl.ds(parity, 128, stride=2), :], parity, row, c_out, values)
                lay(wide[pl.ds(parity, 128, stride=2), :], parity, row, e_out)
    for kind, kappa in enumerate((kappa_east, kappa_north)):
        for level in range(2):
            for parity in range(2):
                lay(kappa[level, pl.ds(parity, 128, stride=2), :], parity, 2 * kind + level, raw)
    for parity in range(2):
        join(raw.at[parity])
        saved[parity, pl.ds(16 * STEPS, 8), :] = raw[parity, tiles(HALO, 1), :]
    coefficients(raw, east, same, other, blocks_from(HALO))

    def save(section, src):
        for parity in range(2):
            saved[parity, pl.ds(16 * section, 16), :] = src[parity, tiles(HALO + section, 2), :]

    diffuse(values, spare, east, same, other, inward(HALO), before_step=save)
    multiply(values, e_out, product, blocks_from(HALO))


def copy_of(source, target, sem):
    return pltpu.make_async_copy(source, target, sem)


def received(near, far, at):
    odd = lax.axis_index("lon") % 2 == 1
    one, two = (part[8 * at : 8 * (at + 1), :].reshape(1, 8, 128) for part in (near, far))
    return jnp.where(odd, two, one), jnp.where(odd, one, two)


def outer(near, far, at, width, *outs):
    low = row_index() < 4
    for place in range(HALO - width, HALO):
        one, two = received(near, far, at)
        even = jnp.where(low, one, pltpu.roll(two, 4, 1))
        odd = jnp.where(low, pltpu.roll(one, 4, 1), two)
        for out in outs:
            put(out.at[0], place, even)
            put(out.at[1], place, odd)
        at += 1


def block_rows(chip, own):
    core = lax.axis_index("mem") % 2
    if not own:
        core = 1 - core
    return pl.ds(pl.multiple_of(16 * chip + 8 * core, 8), 8)


def lay_out(product, plain, mine, other_core):
    for parity in range(2):
        edges = []
        for level in range(2):
            plain[level, pl.ds(parity, 128, stride=2), :] = band_of(product.at[parity], level).T
            for half in range(2):
                edges.append(product[parity, rows(0, level + 4 * half, 32), :])
        plain[2, pl.ds(parity, 128, stride=2), :] = jnp.concatenate(edges, axis=0).T
    for tile in range(3):
        for chip in range(mine.shape[0]):
            mine[chip, tile] = plain[tile, block_rows(chip, True), :]
            other_core[chip, tile] = plain[tile, block_rows(chip, False), :]


def spread(mine, other_core, plain, forcing):
    for tile in range(3):
        for chip in range(mine.shape[0]):
            plain[tile, block_rows(chip, True), :] = mine[chip, tile]
            plain[tile, block_rows(chip, False), :] = other_core[chip, tile]
    for parity in range(2):
        edges = plain[2, pl.ds(parity, 128, stride=2), :].T
        for level in range(2):
            halves = halves_of(plain[level, pl.ds(parity, 128, stride=2), :].T)
            for half in range(2):
                edge = edges[64 * level + 32 * half : 64 * level + 32 * half + HALO]
                for member in range(2):
                    row = 4 * half + 2 * member + level
                    forcing[parity, rows(0, row, HALO), :] = edge
                    forcing[parity, rows(HALO, row, 64), :] = halves[half]


def outer_kernel(near, far, w_in, i_in, saved, e_hbm, east_hbm, same_hbm, other_hbm, product_hbm,
                 mine, other_core, w_out, i_out, c_far, e_far, east_far, same_far, other_far,
                 values, spare, plain, product, raw, c, e, east, same, other, sem_in, sem_out):
    edge, rest = tiles(HALO, UNIT), tiles(HALO + STEPS, SPAN - HALO - STEPS)
    fetched = [
        copy_of(source.at[..., edge, :], target.at[..., edge, :], sem_in.at[place])
        for place, (source, target) in enumerate(((e_hbm, e), (east_hbm, east), (same_hbm, same), (other_hbm, other)))
    ]
    fetched.append(copy_of(product_hbm.at[:, rest, :], product.at[:, rest, :], sem_in.at[4]))
    for copy in fetched:
        copy.start()
    outer(near, far, HALO, HALO, raw)
    for parity in range(2):
        raw[parity, tiles(HALO, 1), :] = saved[parity, pl.ds(16 * STEPS, 8), :]
    outer(near, far, 0, HALO, c, values)
    outer(near, far, 2 * HALO, REACH, e)
    for row, (band, result) in enumerate(((w_in, w_out), (i_in, i_out))):
        at = 2 * HALO + REACH + row
        result[:2] = band[...]
        result[2] = near[8 * at : 8 * (at + 1), :] + far[8 * at : 8 * (at + 1), :]
    coefficients(raw, east, same, other, range(0, HALO, UNIT))
    places = tiles(0, HALO)
    kept = [
        copy_of(source.at[..., places, :], target, sem_out.at[place])
        for place, (source, target) in enumerate(
            ((c, c_far), (e, e_far), (east, east_far), (same, same_far), (other, other_far))
        )
    ]
    for copy in kept:
        copy.start()
    for copy in fetched[:4]:
        copy.wait()

    def complete(section, src):
        for parity in range(2):
            src[parity, tiles(HALO + section, 2), :] = saved[parity, pl.ds(16 * section, 16), :]

    spans = [(step, step + HALO) for step in range(1, STEPS + 1)]
    diffuse(values, spare, east, same, other, spans, joined=False, before_step=complete)
    fetched[4].wait()
    multiply(values, e, product, range(STEPS, STEPS + HALO, UNIT))
    lay_out(product, plain, mine, other_core)
    for copy in kept:
        copy.wait()


def forcing_kernel(parts, weight, innovation, out, *increment, scale):
    total = parts[0]
    for block in range(1, parts.shape[0]):
        total = total + parts[block]
    total = scale * total
    if increment:
        increment[0][...] = total[:2]
    forcing = weight[...] * (total - innovation[...])
    for block in range(out.shape[0]):
        out[block] = forcing


def fetch(sources, targets, sems):
    inside, outside = tiles(HALO, SPAN - HALO), tiles(0, HALO)
    waits = []
    for place, (target, (inner, far)) in enumerate(zip(targets, sources)):
        pair = (
            copy_of(inner.at[..., inside, :], target.at[..., inside, :], sems.at[2 * place]),
            copy_of(far, target.at[..., outside, :], sems.at[2 * place + 1]),
        )
        for copy in pair:
            copy.start()
        waits.append(pair)

    def wait(place):
        for copy in waits[place]:
            copy.wait()

    return wait


def gradient(wait, e, east, same, other, values, spare, scale, lo):
    wait(0)
    for at in blocks_from(lo):
        for parity in range(2):
            term = get(e.at[parity], at, UNIT) * get(values.at[parity], at, UNIT)
            put(values.at[parity], at, scale * term)
    for place in (1, 2, 3):
        wait(place)
    diffuse(values, spare, east, same, other, inward(lo))


def middle_kernel(mine, other_core, e_in, e_far, east_in, east_far, same_in, same_far, other_in, other_far,
                  c_in, c_far, mine_out, other_out, c_hbm,
                  values, spare, plain, e, east, same, other, c, c_new, sems, sem_out, *, scale):
    sources = ((e_in, e_far), (east_in, east_far), (same_in, same_far), (other_in, other_far), (c_in, c_far))
    wait = fetch(sources, (e, east, same, other, c), sems)
    spread(mine, other_core, plain, values)
    gradient(wait, e, east, same, other, values, spare, scale, STEPS)
    wait(4)
    for at in blocks_from(2 * STEPS):
        for parity in range(2):
            new = get(c.at[parity], at, UNIT)
            new = new - step_size * (new + get(values.at[parity], at, UNIT))
            put(c_new.at[parity], at, new)
            put(values.at[parity], at, new)
    inside = tiles(HALO, SPAN - HALO)
    keep = copy_of(c_new.at[:, inside, :], c_hbm, sem_out)
    keep.start()
    diffuse(values, spare, east, same, other, inward(2 * STEPS))
    multiply(values, e, spare, blocks_from(3 * STEPS))
    lay_out(spare, plain, mine_out, other_out)
    keep.wait()


def last_kernel(mine, other_core, e_in, e_far, east_in, east_far, same_in, same_far, other_in, other_far,
                c_in, out_hbm, values, spare, plain, e, east, same, other, c, out, sems, sem_in, sem_out, *, scale):
    inside = tiles(HALO, SPAN - HALO)
    last = copy_of(c_in, c.at[:, inside, :], sem_in)
    sources = ((e_in, e_far), (east_in, east_far), (same_in, same_far), (other_in, other_far))
    wait = fetch(sources, (e, east, same, other), sems)
    last.start()
    spread(mine, other_core, plain, values)
    gradient(wait, e, east, same, other, values, spare, scale, 3 * STEPS)
    last.wait()
    for at in blocks_from(HALO):
        for parity in range(2):
            new = get(c.at[parity], at, UNIT)
            put(values.at[parity], at, new - step_size * (new + get(values.at[parity], at, UNIT)))
    copies = []
    for member in range(2):
        for level in range(2):
            for parity in range(2):
                part = band_of(values.at[parity], 2 * member + level)
                out[member, level, pl.ds(parity, 128, stride=2), :] = part.T
            copy = copy_of(out.at[member, level], out_hbm.at[member, level], sem_out.at[2 * member + level])
            copy.start()
            copies.append(copy)
    for copy in copies:
        copy.wait()


def near_core(value):
    return pltpu.with_memory_space_constraint(value, pltpu.VMEM)


def call(kernel, outs, scratch, name, *args, far_in=(), far_out=()):
    here, far = pl.BlockSpec(memory_space=pltpu.VMEM), pl.BlockSpec(memory_space=pl.ANY)
    copied = not all(isinstance(part, tuple) for part in scratch)
    return pl.pallas_call(
        kernel,
        out_shape=[
            (jax.ShapeDtypeStruct if place in far_out else pltpu.VMEM)(shape, jnp.float32)
            for place, shape in enumerate(outs)
        ],
        in_specs=[far if place in far_in else here for place in range(len(args))],
        out_specs=[far if place in far_out and copied else here for place in range(len(outs))],
        scratch_shapes=[pltpu.VMEM(part, jnp.float32) if isinstance(part, tuple) else part for part in scratch],
        name=name,
    )(*args)


def swap_chips(parts):
    size = lax.axis_size("mem")
    groups = [list(range(core, size, 2)) for core in range(2)]
    return lax.all_to_all(parts, "mem", split_axis=0, concat_axis=0, tiled=True, axis_index_groups=groups)


def swap_cores(part):
    return lax.ppermute(part, "mem", [(i, i ^ 1) for i in range(lax.axis_size("mem"))])


def swap_bands(part, odd_up):
    bands = lax.axis_size("lon")
    return lax.ppermute(part, "lon", [(i, (i + 1 if (i % 2 == 1) == odd_up else i - 1) % bands) for i in range(bands)])


def body(ensemble, controls_start, kappa_east, kappa_north, innovation, obs_mask, gauge_index, gauge_precision):
    chips = lax.axis_size("mem") // 2
    scale = float(lax.axis_size("mem") * ensemble.shape[0]) ** (-0.5)
    field, one, plain = (2, 8 * SIZE, 128), (8 * SIZE, 128), (3, 256, 128)
    far_field, far_one, band = (2, 8 * HALO, 128), (8 * HALO, 128), (2, 8 * (SPAN - HALO), 128)
    parcel, parts, local, wide = (8 * SENT, 128), (chips, 3, 8, 128), (3, 8, 128), (256, 128)
    sem = pltpu.SemaphoreType.DMA
    w, innov, first, second = call(
        edges_kernel, (innovation.shape, innovation.shape, parcel, parcel), (parcel, parcel, wide), "edges",
        controls_start, ensemble, kappa_east, kappa_north, innovation, obs_mask, gauge_index,
        gauge_precision.reshape(1, GAUGES),
    )
    near, far = near_core(swap_bands(first, True)), near_core(swap_bands(second, False))
    c, e, east, same, other, product, saved = call(
        inner_kernel, (field, field, field, one, one, field, (2, 8 * (2 * STEPS + 1), 128)), (field, field, field, wide),
        "inner", controls_start, ensemble, kappa_east, kappa_north, far_out=range(6),
    )
    w, innov, saved = near_core(w), near_core(innov), near_core(saved)
    mine, theirs, weight, innov, c_far, e_far, east_far, same_far, other_far = call(
        outer_kernel, (parts, parts, local, local, far_field, far_field, far_field, far_one, far_one),
        (field, field, plain, field, field, field, field, field, one, one, sem((5,)), sem((5,))), "outer",
        near, far, w, innov, saved, e, east, same, other, product, far_in=range(5, 10), far_out=range(4, 9),
    )
    weight, innov = near_core(weight), near_core(innov)
    fixed = (e, e_far, east, east_far, same, same_far, other, other_far)

    def forced(mine, theirs, outs):
        kernel = lambda *refs: forcing_kernel(*refs, scale=scale)
        sums = near_core(swap_chips(mine + swap_cores(theirs)))
        forcing, *increment = call(kernel, outs, (), "forcing", sums, weight, innov)
        mine = swap_chips(forcing)
        return near_core(mine), near_core(swap_cores(mine)), *increment

    mine, theirs = forced(mine, theirs, (parts,))
    kernel = lambda *refs: middle_kernel(*refs, scale=scale)
    mine, theirs, c = call(
        kernel, (parts, parts, band), (field, field, plain, field, field, one, one, field, field, sem((10,)), sem),
        "middle", mine, theirs, *fixed, c, c_far, far_in=range(2, 12), far_out=(2,),
    )
    mine, theirs, increment = forced(mine, theirs, (parts, innovation.shape))
    kernel = lambda *refs: last_kernel(*refs, scale=scale)
    (controls,) = call(
        kernel, (controls_start.shape,),
        (field, field, plain, field, field, one, one, field, controls_start.shape, sem((8,)), sem, sem((4,))),
        "last", mine, theirs, *fixed, c, far_in=range(2, 11), far_out=(0,),
    )
    return controls, increment


def solution(mesh):
    in_specs = (
        P("mem", None, None, "lon"),
        P("mem", None, None, "lon"),
        P(None, None, "lon"),
        P(None, None, "lon"),
        P(None, "mem", "lon"),
        P(None, "mem", "lon"),
        P(None, "mem", "lon"),
        P(),
    )
    out_specs = (P("mem", None, None, "lon"), P(None, "mem", "lon"))
    return jax.shard_map(body, mesh=mesh, in_specs=in_specs, out_specs=out_specs, check_vma=False)
```

```python
import jax
import jax.numpy as jnp
from jax import lax
from jax.experimental import pallas as pl
from jax.experimental.pallas import tpu as pltpu
from jax.sharding import PartitionSpec as P

STEPS = 6
GAUGES = 64
step_size = 0.5

BAND = 128
PAD = 1
HALO = 4 * STEPS
REACH = 3 * STEPS
SPAN = HALO + BAND // 2
SIZE = PAD + SPAN + PAD
UNIT = 8
LEAD, LAG = 6, 6
SENT = 2 * HALO + REACH + 2


def tiles(place, count):
    if isinstance(place, int):
        return pl.ds(8 * (PAD + place), 8 * count)
    return pl.ds(pl.multiple_of(8 * (PAD + place), 8), 8 * count)


def get(ref, place, count):
    return ref[tiles(place, count), :].reshape(count, 8, 128)


def put(ref, place, value):
    ref[tiles(place, value.shape[0]), :] = value.reshape(-1, 128)


def rows(place, row, count):
    return pl.ds(8 * (PAD + place) + row, count, stride=8)


def lane_index():
    return lax.broadcasted_iota(jnp.int32, (1, 8, 128), 2)


def row_index():
    return lax.broadcasted_iota(jnp.int32, (1, 8, 128), 1)


def flipped(value):
    groups = value.reshape(-1, 8, 128)
    index = 7 - lax.broadcasted_iota(jnp.int32, groups.shape, 1)
    groups = jnp.take_along_axis(groups, index, axis=1)
    count = groups.shape[0]
    return jnp.concatenate([groups[count - 1 - i] for i in range(count)], axis=0)


def halves_of(band):
    return band[:64], flipped(band[64:])


def band_of(ref, row):
    first = ref[rows(HALO, row, 64), :]
    return jnp.concatenate([first, flipped(ref[rows(HALO, row + 4, 64), :])], axis=0)


def blocks_from(lo, hi=SPAN):
    return range(hi - UNIT * -(-(hi - lo) // UNIT), hi, UNIT)


def join(ref):
    put(ref, SPAN, pltpu.roll(get(ref, SPAN - 1, 1), 4, 1))


def diffuse(source, spare, east, same, other, spans, joined=True, before_step=None):
    if joined:
        for parity in range(2):
            join(source.at[parity])
    stream = [(section, place) for section, (first, end) in enumerate(spans) for place in range(first, end)]
    ends = (source, spare)
    ahead, open_places, before, values = {}, {}, [None, None], [None, None]

    def turn(item):
        section, place = stream[item]
        ahead[item] = pltpu.roll(get(ends[section % 2].at[0], place, 1), 127, 2)

    def finish(item):
        section, place = stream[item]
        dst = ends[(section + 1) % 2]
        part, back = open_places.pop(item)
        put(dst.at[0], place, part - back)
        if joined and place == SPAN - 1:
            for parity in range(2):
                join(dst.at[parity])

    for item in range(LEAD):
        turn(item)
    for item, (section, place) in enumerate(stream):
        src, dst = ends[section % 2], ends[(section + 1) % 2]
        if place == spans[section][0]:
            if before_step is not None:
                before_step(section, src)
            for parity in range(2):
                values[parity] = get(src.at[parity], place, 1)
                face = values[parity] - get(src.at[parity], place - 1, 1)
                before[parity] = get(east.at[parity], place - 1, 1) * face
        if item + LEAD < len(stream):
            turn(item + LEAD)
        even, odd = values
        across = get(other, place, 1) * (ahead.pop(item) - odd)
        back = pltpu.roll(across, 1, 2)
        within = get(same, place, 1) * (odd - even)
        for parity, north in ((0, within), (1, across - within)):
            after = get(src.at[parity], place + 1, 1)
            flux = get(east.at[parity], place, 1) * (after - values[parity])
            new = (values[parity] + (flux - before[parity])) + north
            before[parity], values[parity] = flux, after
            if parity:
                put(dst.at[1], place, new)
            else:
                open_places[item] = (new, back)
        if item >= LAG:
            finish(item - LAG)
    for item in range(len(stream) - LAG, len(stream)):
        finish(item)


def inward(lo):
    return [(blocks_from(lo + step)[0], SPAN) for step in range(1, STEPS + 1)]


def edges_kernel(controls, ensemble, kappa_east, kappa_north, innovation, mask, gauge, precision,
                 w_out, i_out, first, second, right, left, wide):
    odd = lax.axis_index("lon") % 2 == 1

    def send(values, at, row):
        turned = values.T
        right[pl.ds(8 * at + row, HALO, stride=8), :] = turned[BAND - HALO :]
        left[pl.ds(8 * at + row, HALO, stride=8), :] = flipped(turned[:HALO])

    for member in range(2):
        for level in range(2):
            row = 2 * member + level
            wide[row] = ensemble[member, level].astype(jnp.float32)
            for parity in range(2):
                send(controls[member, level, pl.ds(parity, 128, stride=2), :], 0, 4 * parity + row)
                send(wide[row, pl.ds(parity, 128, stride=2), :], HALO + REACH, 4 * parity + row)
    for kind, kappa in enumerate((kappa_east, kappa_north)):
        for level in range(2):
            for parity in range(2):
                send(kappa[level, pl.ds(parity, 128, stride=2), :], HALO, 4 * parity + 2 * kind + level)
    index = gauge[...]
    found = jnp.zeros(index.shape, jnp.float32)
    for label in range(GAUGES):
        found = jnp.where(index == label, precision[0, label], found)
    weight = found * mask[...].astype(jnp.float32)
    w_out[...] = weight
    i_out[...] = innovation[...]
    lanes = lax.broadcasted_iota(jnp.int32, (8, 128), 1)
    at = 2 * HALO + REACH
    for value in (weight, innovation[...]):
        to_right = jnp.zeros((8, 128), jnp.float32)
        to_left = jnp.zeros((8, 128), jnp.float32)
        for level in range(2):
            place = lanes - 64 * level
            moved = jnp.take_along_axis(value[level], jnp.clip(BAND - HALO + place, 0, 127), axis=1)
            to_right = jnp.where((place >= HALO - REACH) & (place < HALO), moved, to_right)
            place = place - 32
            moved = jnp.take_along_axis(value[level], jnp.clip(HALO - 1 - place, 0, 127), axis=1)
            to_left = jnp.where((place >= HALO - REACH) & (place < HALO), moved, to_left)
        right[8 * at : 8 * (at + 1), :] = to_right
        left[8 * at : 8 * (at + 1), :] = to_left
        at += 1
    first[...] = jnp.where(odd, right[...], left[...])
    second[...] = jnp.where(odd, left[...], right[...])


def coefficients(raw, east, same, other, blocks):
    low = row_index() < 4
    second = row_index() % 4 >= 2
    last = lane_index() == 127
    for at in blocks:
        for parity in range(2):
            both = get(raw.at[parity], at, UNIT + 1)
            face = jnp.where(low, both[:-1], both[1:])
            put(east.at[parity], at, jnp.where(second, pltpu.roll(face, 2, 1), face))
            north = jnp.where(second, both[:-1], pltpu.roll(both[:-1], 6, 1))
            if parity == 0:
                put(same, at, north)
            else:
                put(other, at, jnp.where(last, 0.0, north))


def multiply(values, ensemble, product, blocks):
    for at in blocks:
        for parity in range(2):
            term = get(ensemble.at[parity], at, UNIT) * get(values.at[parity], at, UNIT)
            put(product.at[parity], at, term + pltpu.roll(term, 6, 1))


def inner_kernel(controls, ensemble, kappa_east, kappa_north,
                 c_out, e_out, east, same, other, product, saved, values, spare, raw, wide):
    def lay(values, parity, row, *outs):
        for half, part in enumerate(halves_of(values.T)):
            for out in outs:
                out[parity, rows(HALO, row + 4 * half, 64), :] = part

    for member in range(2):
        for level in range(2):
            row = 2 * member + level
            wide[row] = ensemble[member, level].astype(jnp.float32)
            for parity in range(2):
                lay(controls[member, level, pl.ds(parity, 128, stride=2), :], parity, row, c_out, values)
                lay(wide[row, pl.ds(parity, 128, stride=2), :], parity, row, e_out)
    for kind, kappa in enumerate((kappa_east, kappa_north)):
        for level in range(2):
            for parity in range(2):
                lay(kappa[level, pl.ds(parity, 128, stride=2), :], parity, 2 * kind + level, raw)
    for parity in range(2):
        join(raw.at[parity])
        saved[parity, pl.ds(16 * STEPS, 8), :] = raw[parity, tiles(HALO, 1), :]
    coefficients(raw, east, same, other, blocks_from(HALO))

    def save(section, src):
        for parity in range(2):
            saved[parity, pl.ds(16 * section, 16), :] = src[parity, tiles(HALO + section, 2), :]

    diffuse(values, spare, east, same, other, inward(HALO), before_step=save)
    multiply(values, e_out, product, blocks_from(HALO))


def copy_of(source, target, sem):
    return pltpu.make_async_copy(source, target, sem)


def received(near, far, at):
    odd = lax.axis_index("lon") % 2 == 1
    one, two = (part[8 * at : 8 * (at + 1), :].reshape(1, 8, 128) for part in (near, far))
    return jnp.where(odd, two, one), jnp.where(odd, one, two)


def outer(near, far, at, width, *outs):
    low = row_index() < 4
    for place in range(HALO - width, HALO):
        one, two = received(near, far, at)
        even = jnp.where(low, one, pltpu.roll(two, 4, 1))
        odd = jnp.where(low, pltpu.roll(one, 4, 1), two)
        for out in outs:
            put(out.at[0], place, even)
            put(out.at[1], place, odd)
        at += 1


def own_rows():
    core = lax.axis_index("mem") % 2
    return (row_index()[0] < 4) == (core == 0)


def grouped(block):
    place = lax.broadcasted_iota(jnp.int32, block.shape, block.ndim - 2)
    block = jnp.take_along_axis(block, (2 * place) % 8 + place // 4, axis=block.ndim - 2)
    core = lax.axis_index("mem") % 2
    return jnp.where(core == 0, block, pltpu.roll(block, 4, block.ndim - 2))


def ungrouped(block):
    core = lax.axis_index("mem") % 2
    block = jnp.where(core == 0, block, pltpu.roll(block, 4, block.ndim - 2))
    place = lax.broadcasted_iota(jnp.int32, block.shape, block.ndim - 2)
    return jnp.take_along_axis(block, place // 2 + 4 * (place % 2), axis=block.ndim - 2)


def lay_out(product, mine, other_core):
    own = own_rows()
    for tile in range(3):
        turned = []
        for parity in range(2):
            if tile < 2:
                part = band_of(product.at[parity], tile)
            else:
                part = jnp.concatenate(
                    [product[parity, rows(0, level + 4 * half, 32), :] for level in range(2) for half in range(2)],
                    axis=0,
                )
            turned.append(part.T)
        even, odd = turned
        for chip in range(mine.shape[0]):
            here = slice(8 * chip, 8 * (chip + 1))
            other = pltpu.roll(odd[here], 4, 0)
            mine[chip, tile] = jnp.where(own, even[here], other)
            other_core[chip, tile] = jnp.where(own, other, even[here])


def spread(mine, other_core, forcing):
    own = own_rows()
    for tile in range(3):
        parts = ([], [])
        for chip in range(mine.shape[0]):
            one, two = mine[chip, tile], other_core[chip, tile]
            parts[0].append(jnp.where(own, one, two))
            parts[1].append(pltpu.roll(jnp.where(own, two, one), 4, 0))
        for parity in range(2):
            turned = jnp.concatenate(parts[parity], axis=0).T
            if tile < 2:
                pieces = [(tile, half, HALO, part) for half, part in enumerate(halves_of(turned))]
            else:
                pieces = [
                    (level, half, 0, turned[64 * level + 32 * half : 64 * level + 32 * half + HALO])
                    for level in range(2)
                    for half in range(2)
                ]
            for level, half, place, part in pieces:
                for member in range(2):
                    row = 4 * half + 2 * member + level
                    forcing[parity, rows(place, row, part.shape[0]), :] = part


def outer_kernel(near, far, w_in, i_in, saved, e_hbm, east_hbm, same_hbm, other_hbm, product_hbm,
                 mine, other_core, w_out, i_out, c_far, e_far, east_far, same_far, other_far,
                 values, spare, product, raw, c, e, east, same, other, sem_in, sem_out):
    edge, rest = tiles(HALO, UNIT), tiles(HALO + STEPS, SPAN - HALO - STEPS)
    fetched = [
        copy_of(source.at[..., edge, :], target.at[..., edge, :], sem_in.at[place])
        for place, (source, target) in enumerate(((e_hbm, e), (east_hbm, east), (same_hbm, same), (other_hbm, other)))
    ]
    fetched.append(copy_of(product_hbm.at[:, rest, :], product.at[:, rest, :], sem_in.at[4]))
    for copy in fetched:
        copy.start()
    outer(near, far, HALO, HALO, raw)
    for parity in range(2):
        raw[parity, tiles(HALO, 1), :] = saved[parity, pl.ds(16 * STEPS, 8), :]
    outer(near, far, 0, HALO, c, values)
    outer(near, far, 2 * HALO, REACH, e)
    for row, (band, result) in enumerate(((w_in, w_out), (i_in, i_out))):
        at = 2 * HALO + REACH + row
        result[:2] = band[...]
        result[2] = near[8 * at : 8 * (at + 1), :] + far[8 * at : 8 * (at + 1), :]
    coefficients(raw, east, same, other, range(0, HALO, UNIT))
    places = tiles(0, HALO)
    kept = [
        copy_of(source.at[..., places, :], target, sem_out.at[place])
        for place, (source, target) in enumerate(
            ((c, c_far), (e, e_far), (east, east_far), (same, same_far), (other, other_far))
        )
    ]
    for copy in kept:
        copy.start()
    for copy in fetched[:4]:
        copy.wait()

    def complete(section, src):
        for parity in range(2):
            src[parity, tiles(HALO + section, 2), :] = saved[parity, pl.ds(16 * section, 16), :]

    spans = [(step, step + HALO) for step in range(1, STEPS + 1)]
    diffuse(values, spare, east, same, other, spans, joined=False, before_step=complete)
    fetched[4].wait()
    multiply(values, e, product, range(STEPS, STEPS + HALO, UNIT))
    lay_out(product, mine, other_core)
    for copy in kept:
        copy.wait()


def forcing_kernel(parts, weight, innovation, out, *increment, scale):
    total = parts[0]
    for block in range(1, parts.shape[0]):
        total = total + parts[block]
    total = ungrouped(scale * total)
    if increment:
        increment[0][...] = total[:2]
    forcing = grouped(weight[...] * (total - innovation[...]))
    for block in range(out.shape[0]):
        out[block] = forcing


def fetch(sources, targets, sems):
    inside, outside = tiles(HALO, SPAN - HALO), tiles(0, HALO)
    waits = []
    for place, (target, (inner, far)) in enumerate(zip(targets, sources)):
        pair = (
            copy_of(inner.at[..., inside, :], target.at[..., inside, :], sems.at[2 * place]),
            copy_of(far, target.at[..., outside, :], sems.at[2 * place + 1]),
        )
        for copy in pair:
            copy.start()
        waits.append(pair)

    def wait(place):
        for copy in waits[place]:
            copy.wait()

    return wait


def gradient(wait, e, east, same, other, values, spare, scale, lo):
    wait(0)
    for at in blocks_from(lo):
        for parity in range(2):
            term = get(e.at[parity], at, UNIT) * get(values.at[parity], at, UNIT)
            put(values.at[parity], at, scale * term)
    for place in (1, 2, 3):
        wait(place)
    diffuse(values, spare, east, same, other, inward(lo))


def middle_kernel(mine, other_core, e_in, e_far, east_in, east_far, same_in, same_far, other_in, other_far,
                  c_in, c_far, mine_out, other_out, c_hbm,
                  values, spare, e, east, same, other, c, c_new, sems, sem_out, *, scale):
    sources = ((e_in, e_far), (east_in, east_far), (same_in, same_far), (other_in, other_far), (c_in, c_far))
    wait = fetch(sources, (e, east, same, other, c), sems)
    spread(mine, other_core, values)
    gradient(wait, e, east, same, other, values, spare, scale, STEPS)
    wait(4)
    for at in blocks_from(2 * STEPS):
        for parity in range(2):
            new = get(c.at[parity], at, UNIT)
            new = new - step_size * (new + get(values.at[parity], at, UNIT))
            put(c_new.at[parity], at, new)
            put(values.at[parity], at, new)
    inside = tiles(HALO, SPAN - HALO)
    keep = copy_of(c_new.at[:, inside, :], c_hbm, sem_out)
    keep.start()
    diffuse(values, spare, east, same, other, inward(2 * STEPS))
    multiply(values, e, spare, blocks_from(3 * STEPS))
    lay_out(spare, mine_out, other_out)
    keep.wait()


def last_kernel(mine, other_core, e_in, e_far, east_in, east_far, same_in, same_far, other_in, other_far,
                c_in, out_hbm, values, spare, e, east, same, other, c, out, sems, sem_in, sem_out, *, scale):
    inside = tiles(HALO, SPAN - HALO)
    last = copy_of(c_in, c.at[:, inside, :], sem_in)
    sources = ((e_in, e_far), (east_in, east_far), (same_in, same_far), (other_in, other_far))
    wait = fetch(sources, (e, east, same, other), sems)
    last.start()
    spread(mine, other_core, values)
    gradient(wait, e, east, same, other, values, spare, scale, 3 * STEPS)
    last.wait()
    for at in blocks_from(HALO):
        for parity in range(2):
            new = get(c.at[parity], at, UNIT)
            put(values.at[parity], at, new - step_size * (new + get(values.at[parity], at, UNIT)))
    copies = []
    for member in range(2):
        for level in range(2):
            for parity in range(2):
                part = band_of(values.at[parity], 2 * member + level)
                out[member, level, pl.ds(parity, 128, stride=2), :] = part.T
            copy = copy_of(out.at[member, level], out_hbm.at[member, level], sem_out.at[2 * member + level])
            copy.start()
            copies.append(copy)
    for copy in copies:
        copy.wait()


def near_core(value):
    return pltpu.with_memory_space_constraint(value, pltpu.VMEM)


def call(kernel, outs, scratch, name, *args, far_in=(), far_out=()):
    here, far = pl.BlockSpec(memory_space=pltpu.VMEM), pl.BlockSpec(memory_space=pl.ANY)
    copied = not all(isinstance(part, tuple) for part in scratch)
    return pl.pallas_call(
        kernel,
        out_shape=[
            (jax.ShapeDtypeStruct if place in far_out else pltpu.VMEM)(shape, jnp.float32)
            for place, shape in enumerate(outs)
        ],
        in_specs=[far if place in far_in else here for place in range(len(args))],
        out_specs=[far if place in far_out and copied else here for place in range(len(outs))],
        scratch_shapes=[pltpu.VMEM(part, jnp.float32) if isinstance(part, tuple) else part for part in scratch],
        name=name,
    )(*args)


def swap_chips(parts):
    size = lax.axis_size("mem")
    groups = [list(range(core, size, 2)) for core in range(2)]
    return lax.all_to_all(parts, "mem", split_axis=0, concat_axis=0, tiled=True, axis_index_groups=groups)


def swap_cores(part):
    return lax.ppermute(part, "mem", [(i, i ^ 1) for i in range(lax.axis_size("mem"))])


def swap_bands(part, odd_up):
    bands = lax.axis_size("lon")
    return lax.ppermute(part, "lon", [(i, (i + 1 if (i % 2 == 1) == odd_up else i - 1) % bands) for i in range(bands)])


def body(ensemble, controls_start, kappa_east, kappa_north, innovation, obs_mask, gauge_index, gauge_precision):
    chips = lax.axis_size("mem") // 2
    scale = float(lax.axis_size("mem") * ensemble.shape[0]) ** (-0.5)
    field, one = (2, 8 * SIZE, 128), (8 * SIZE, 128)
    far_field, far_one, band = (2, 8 * HALO, 128), (8 * HALO, 128), (2, 8 * (SPAN - HALO), 128)
    parcel, parts, local, wide = (8 * SENT, 128), (chips, 3, 8, 128), (3, 8, 128), (4, 256, 128)
    sem = pltpu.SemaphoreType.DMA
    w, innov, first, second = call(
        edges_kernel, (innovation.shape, innovation.shape, parcel, parcel), (parcel, parcel, wide), "edges",
        controls_start, ensemble, kappa_east, kappa_north, innovation, obs_mask, gauge_index,
        gauge_precision.reshape(1, GAUGES),
    )
    near, far = near_core(swap_bands(first, True)), near_core(swap_bands(second, False))
    c, e, east, same, other, product, saved = call(
        inner_kernel, (field, field, field, one, one, field, (2, 8 * (2 * STEPS + 1), 128)), (field, field, field, wide),
        "inner", controls_start, ensemble, kappa_east, kappa_north, far_out=range(6),
    )
    w, innov, saved = near_core(w), near_core(innov), near_core(saved)
    mine, theirs, weight, innov, c_far, e_far, east_far, same_far, other_far = call(
        outer_kernel, (parts, parts, local, local, far_field, far_field, far_field, far_one, far_one),
        (field, field, field, field, field, field, field, one, one, sem((5,)), sem((5,))), "outer",
        near, far, w, innov, saved, e, east, same, other, product, far_in=range(5, 10), far_out=range(4, 9),
    )
    weight, innov = near_core(weight), near_core(innov)
    fixed = (e, e_far, east, east_far, same, same_far, other, other_far)

    def forced(mine, theirs, outs):
        kernel = lambda *refs: forcing_kernel(*refs, scale=scale)
        sums = near_core(swap_chips(mine + swap_cores(theirs)))
        forcing, *increment = call(kernel, outs, (), "forcing", sums, weight, innov)
        mine = swap_chips(forcing)
        return near_core(mine), near_core(swap_cores(mine)), *increment

    mine, theirs = forced(mine, theirs, (parts,))
    kernel = lambda *refs: middle_kernel(*refs, scale=scale)
    mine, theirs, c = call(
        kernel, (parts, parts, band), (field, field, field, field, one, one, field, field, sem((10,)), sem),
        "middle", mine, theirs, *fixed, c, c_far, far_in=range(2, 12), far_out=(2,),
    )
    mine, theirs, increment = forced(mine, theirs, (parts, innovation.shape))
    kernel = lambda *refs: last_kernel(*refs, scale=scale)
    (controls,) = call(
        kernel, (controls_start.shape,),
        (field, field, field, field, one, one, field, controls_start.shape, sem((8,)), sem, sem((4,))),
        "last", mine, theirs, *fixed, c, far_in=range(2, 11), far_out=(0,),
    )
    return controls, increment


def solution(mesh):
    in_specs = (
        P("mem", None, None, "lon"),
        P("mem", None, None, "lon"),
        P(None, None, "lon"),
        P(None, None, "lon"),
        P(None, "mem", "lon"),
        P(None, "mem", "lon"),
        P(None, "mem", "lon"),
        P(),
    )
    out_specs = (P("mem", None, None, "lon"), P(None, "mem", "lon"))
    return jax.shard_map(body, mesh=mesh, in_specs=in_specs, out_specs=out_specs, check_vma=False)
```

```python
import jax
import jax.numpy as jnp
from jax import lax
from jax.experimental import pallas as pl
from jax.experimental.pallas import tpu as pltpu
from jax.sharding import PartitionSpec as P

STEPS = 6
GAUGES = 64
step_size = 0.5

BAND = 128
PAD = 1
HALO = 4 * STEPS
REACH = 3 * STEPS
SPAN = HALO + BAND // 2
SIZE = PAD + SPAN + PAD
UNIT = 8
LEAD, LAG = 6, 6
SENT = 2 * HALO + REACH + 2


def tiles(place, count):
    if isinstance(place, int):
        return pl.ds(8 * (PAD + place), 8 * count)
    return pl.ds(pl.multiple_of(8 * (PAD + place), 8), 8 * count)


def get(ref, place, count):
    return ref[tiles(place, count), :].reshape(count, 8, 128)


def put(ref, place, value):
    ref[tiles(place, value.shape[0]), :] = value.reshape(-1, 128)


def rows(place, row, count):
    return pl.ds(8 * (PAD + place) + row, count, stride=8)


def lane_index():
    return lax.broadcasted_iota(jnp.int32, (1, 8, 128), 2)


def row_index():
    return lax.broadcasted_iota(jnp.int32, (1, 8, 128), 1)


def flipped(value):
    groups = value.reshape(-1, 8, 128)
    index = 7 - lax.broadcasted_iota(jnp.int32, groups.shape, 1)
    groups = jnp.take_along_axis(groups, index, axis=1)
    count = groups.shape[0]
    return jnp.concatenate([groups[count - 1 - i] for i in range(count)], axis=0)


def halves_of(band):
    return band[:64], flipped(band[64:])


def band_of(ref, row):
    first = ref[rows(HALO, row, 64), :]
    return jnp.concatenate([first, flipped(ref[rows(HALO, row + 4, 64), :])], axis=0)


def blocks_from(lo, hi=SPAN):
    return range(hi - UNIT * -(-(hi - lo) // UNIT), hi, UNIT)


def join(ref):
    put(ref, SPAN, pltpu.roll(get(ref, SPAN - 1, 1), 4, 1))


def diffuse(source, spare, east, same, other, spans, joined=True, before_step=None):
    if joined:
        for parity in range(2):
            join(source.at[parity])
    stream = [(section, place) for section, (first, end) in enumerate(spans) for place in range(first, end)]
    ends = (source, spare)
    ahead, open_places, before, values = {}, {}, [None, None], [None, None]

    def turn(item):
        section, place = stream[item]
        ahead[item] = pltpu.roll(get(ends[section % 2].at[0], place, 1), 127, 2)

    def finish(item):
        section, place = stream[item]
        dst = ends[(section + 1) % 2]
        part, back = open_places.pop(item)
        put(dst.at[0], place, part - back)
        if joined and place == SPAN - 1:
            for parity in range(2):
                join(dst.at[parity])

    for item in range(LEAD):
        turn(item)
    for item, (section, place) in enumerate(stream):
        src, dst = ends[section % 2], ends[(section + 1) % 2]
        if place == spans[section][0]:
            if before_step is not None:
                before_step(section, src)
            for parity in range(2):
                values[parity] = get(src.at[parity], place, 1)
                face = values[parity] - get(src.at[parity], place - 1, 1)
                before[parity] = get(east.at[parity], place - 1, 1) * face
        if item + LEAD < len(stream):
            turn(item + LEAD)
        even, odd = values
        across = get(other, place, 1) * (ahead.pop(item) - odd)
        back = pltpu.roll(across, 1, 2)
        within = get(same, place, 1) * (odd - even)
        for parity, north in ((0, within), (1, across - within)):
            after = get(src.at[parity], place + 1, 1)
            flux = get(east.at[parity], place, 1) * (after - values[parity])
            new = (values[parity] + (flux - before[parity])) + north
            before[parity], values[parity] = flux, after
            if parity:
                put(dst.at[1], place, new)
            else:
                open_places[item] = (new, back)
        if item >= LAG:
            finish(item - LAG)
    for item in range(len(stream) - LAG, len(stream)):
        finish(item)


def inward(lo):
    return [(lo + step, SPAN) for step in range(1, STEPS + 1)]


def edges_kernel(controls, ensemble, kappa_east, kappa_north, innovation, mask, gauge, precision,
                 w_out, i_out, first, second, right, left, wide):
    odd = lax.axis_index("lon") % 2 == 1

    def send(values, at, row):
        turned = values.T
        right[pl.ds(8 * at + row, HALO, stride=8), :] = turned[BAND - HALO :]
        left[pl.ds(8 * at + row, HALO, stride=8), :] = flipped(turned[:HALO])

    for member in range(2):
        for level in range(2):
            row = 2 * member + level
            wide[row] = ensemble[member, level].astype(jnp.float32)
            for parity in range(2):
                send(controls[member, level, pl.ds(parity, 128, stride=2), :], 0, 4 * parity + row)
                send(wide[row, pl.ds(parity, 128, stride=2), :], HALO + REACH, 4 * parity + row)
    for kind, kappa in enumerate((kappa_east, kappa_north)):
        for level in range(2):
            for parity in range(2):
                send(kappa[level, pl.ds(parity, 128, stride=2), :], HALO, 4 * parity + 2 * kind + level)
    index = gauge[...]
    found = jnp.zeros(index.shape, jnp.float32)
    for label in range(GAUGES):
        found = jnp.where(index == label, precision[0, label], found)
    weight = found * mask[...].astype(jnp.float32)
    w_out[...] = weight
    i_out[...] = innovation[...]
    lanes = lax.broadcasted_iota(jnp.int32, (8, 128), 1)
    at = 2 * HALO + REACH
    for value in (weight, innovation[...]):
        to_right = jnp.zeros((8, 128), jnp.float32)
        to_left = jnp.zeros((8, 128), jnp.float32)
        for level in range(2):
            place = lanes - 64 * level
            moved = jnp.take_along_axis(value[level], jnp.clip(BAND - HALO + place, 0, 127), axis=1)
            to_right = jnp.where((place >= HALO - REACH) & (place < HALO), moved, to_right)
            place = place - 32
            moved = jnp.take_along_axis(value[level], jnp.clip(HALO - 1 - place, 0, 127), axis=1)
            to_left = jnp.where((place >= HALO - REACH) & (place < HALO), moved, to_left)
        right[8 * at : 8 * (at + 1), :] = to_right
        left[8 * at : 8 * (at + 1), :] = to_left
        at += 1
    first[...] = jnp.where(odd, right[...], left[...])
    second[...] = jnp.where(odd, left[...], right[...])


def coefficients(raw, east, same, other, blocks):
    low = row_index() < 4
    second = row_index() % 4 >= 2
    last = lane_index() == 127
    for at in blocks:
        for parity in range(2):
            both = get(raw.at[parity], at, UNIT + 1)
            face = jnp.where(low, both[:-1], both[1:])
            put(east.at[parity], at, jnp.where(second, pltpu.roll(face, 2, 1), face))
            north = jnp.where(second, both[:-1], pltpu.roll(both[:-1], 6, 1))
            if parity == 0:
                put(same, at, north)
            else:
                put(other, at, jnp.where(last, 0.0, north))


def multiply(values, ensemble, product, blocks):
    for at in blocks:
        for parity in range(2):
            term = get(ensemble.at[parity], at, UNIT) * get(values.at[parity], at, UNIT)
            put(product.at[parity], at, term + pltpu.roll(term, 6, 1))


def inner_kernel(controls, ensemble, kappa_east, kappa_north,
                 c_out, e_out, east, same, other, product, saved, values, spare, raw, wide):
    def lay(values, parity, row, *outs):
        for half, part in enumerate(halves_of(values.T)):
            for out in outs:
                out[parity, rows(HALO, row + 4 * half, 64), :] = part

    for member in range(2):
        for level in range(2):
            row = 2 * member + level
            wide[row] = ensemble[member, level].astype(jnp.float32)
            for parity in range(2):
                lay(controls[member, level, pl.ds(parity, 128, stride=2), :], parity, row, c_out, values)
                lay(wide[row, pl.ds(parity, 128, stride=2), :], parity, row, e_out)
    for kind, kappa in enumerate((kappa_east, kappa_north)):
        for level in range(2):
            for parity in range(2):
                lay(kappa[level, pl.ds(parity, 128, stride=2), :], parity, 2 * kind + level, raw)
    for parity in range(2):
        join(raw.at[parity])
        saved[parity, pl.ds(16 * STEPS, 8), :] = raw[parity, tiles(HALO, 1), :]
    coefficients(raw, east, same, other, blocks_from(HALO))

    def save(section, src):
        for parity in range(2):
            saved[parity, pl.ds(16 * section, 16), :] = src[parity, tiles(HALO + section, 2), :]

    diffuse(values, spare, east, same, other, inward(HALO), before_step=save)
    multiply(values, e_out, product, blocks_from(HALO))


def copy_of(source, target, sem):
    return pltpu.make_async_copy(source, target, sem)


def received(near, far, at):
    odd = lax.axis_index("lon") % 2 == 1
    one, two = (part[8 * at : 8 * (at + 1), :].reshape(1, 8, 128) for part in (near, far))
    return jnp.where(odd, two, one), jnp.where(odd, one, two)


def outer(near, far, at, width, *outs):
    low = row_index() < 4
    for place in range(HALO - width, HALO):
        one, two = received(near, far, at)
        even = jnp.where(low, one, pltpu.roll(two, 4, 1))
        odd = jnp.where(low, pltpu.roll(one, 4, 1), two)
        for out in outs:
            put(out.at[0], place, even)
            put(out.at[1], place, odd)
        at += 1


def own_rows():
    core = lax.axis_index("mem") % 2
    return (row_index()[0] < 4) == (core == 0)


def grouped(block):
    place = lax.broadcasted_iota(jnp.int32, block.shape, block.ndim - 2)
    block = jnp.take_along_axis(block, (2 * place) % 8 + place // 4, axis=block.ndim - 2)
    core = lax.axis_index("mem") % 2
    return jnp.where(core == 0, block, pltpu.roll(block, 4, block.ndim - 2))


def ungrouped(block):
    core = lax.axis_index("mem") % 2
    block = jnp.where(core == 0, block, pltpu.roll(block, 4, block.ndim - 2))
    place = lax.broadcasted_iota(jnp.int32, block.shape, block.ndim - 2)
    return jnp.take_along_axis(block, place // 2 + 4 * (place % 2), axis=block.ndim - 2)


def lay_out(product, mine, other_core):
    own = own_rows()
    for tile in range(3):
        turned = []
        for parity in range(2):
            if tile < 2:
                part = band_of(product.at[parity], tile)
            else:
                part = jnp.concatenate(
                    [product[parity, rows(0, level + 4 * half, 32), :] for level in range(2) for half in range(2)],
                    axis=0,
                )
            turned.append(part.T)
        even, odd = turned
        for chip in range(mine.shape[0]):
            here = slice(8 * chip, 8 * (chip + 1))
            other = pltpu.roll(odd[here], 4, 0)
            mine[chip, tile] = jnp.where(own, even[here], other)
            other_core[chip, tile] = jnp.where(own, other, even[here])


def spread(mine, other_core, forcing):
    own = own_rows()
    for tile in range(3):
        parts = ([], [])
        for chip in range(mine.shape[0]):
            one, two = mine[chip, tile], other_core[chip, tile]
            parts[0].append(jnp.where(own, one, two))
            parts[1].append(pltpu.roll(jnp.where(own, two, one), 4, 0))
        for parity in range(2):
            turned = jnp.concatenate(parts[parity], axis=0).T
            if tile < 2:
                pieces = [(tile, half, HALO, part) for half, part in enumerate(halves_of(turned))]
            else:
                pieces = [
                    (level, half, 0, turned[64 * level + 32 * half : 64 * level + 32 * half + HALO])
                    for level in range(2)
                    for half in range(2)
                ]
            for level, half, place, part in pieces:
                for member in range(2):
                    row = 4 * half + 2 * member + level
                    forcing[parity, rows(place, row, part.shape[0]), :] = part


def outer_kernel(near, far, w_in, i_in, saved, e_hbm, east_hbm, same_hbm, other_hbm, product_hbm,
                 mine, other_core, w_out, i_out, c_far, e_far, east_far, same_far, other_far,
                 values, spare, product, raw, c, e, east, same, other, sem_in, sem_out):
    edge, rest = tiles(HALO, UNIT), tiles(HALO + STEPS, SPAN - HALO - STEPS)
    fetched = [
        copy_of(source.at[..., edge, :], target.at[..., edge, :], sem_in.at[place])
        for place, (source, target) in enumerate(((e_hbm, e), (east_hbm, east), (same_hbm, same), (other_hbm, other)))
    ]
    fetched.append(copy_of(product_hbm.at[:, rest, :], product.at[:, rest, :], sem_in.at[4]))
    for copy in fetched:
        copy.start()
    outer(near, far, HALO, HALO, raw)
    for parity in range(2):
        raw[parity, tiles(HALO, 1), :] = saved[parity, pl.ds(16 * STEPS, 8), :]
    outer(near, far, 0, HALO, c, values)
    outer(near, far, 2 * HALO, REACH, e)
    for row, (band, result) in enumerate(((w_in, w_out), (i_in, i_out))):
        at = 2 * HALO + REACH + row
        result[:2] = band[...]
        result[2] = near[8 * at : 8 * (at + 1), :] + far[8 * at : 8 * (at + 1), :]
    coefficients(raw, east, same, other, range(0, HALO, UNIT))
    places = tiles(0, HALO)
    kept = [
        copy_of(source.at[..., places, :], target, sem_out.at[place])
        for place, (source, target) in enumerate(
            ((c, c_far), (e, e_far), (east, east_far), (same, same_far), (other, other_far))
        )
    ]
    for copy in kept:
        copy.start()
    for copy in fetched[:4]:
        copy.wait()

    def complete(section, src):
        for parity in range(2):
            src[parity, tiles(HALO + section, 2), :] = saved[parity, pl.ds(16 * section, 16), :]

    spans = [(step, step + HALO) for step in range(1, STEPS + 1)]
    diffuse(values, spare, east, same, other, spans, joined=False, before_step=complete)
    fetched[4].wait()
    multiply(values, e, product, range(STEPS, STEPS + HALO, UNIT))
    lay_out(product, mine, other_core)
    for copy in kept:
        copy.wait()


def forcing_kernel(parts, weight, innovation, out, *increment, scale):
    total = parts[0]
    for block in range(1, parts.shape[0]):
        total = total + parts[block]
    total = ungrouped(scale * total)
    if increment:
        increment[0][...] = total[:2]
    forcing = grouped(weight[...] * (total - innovation[...]))
    for block in range(out.shape[0]):
        out[block] = forcing


def fetch(sources, targets, sems):
    inside, outside = tiles(HALO, SPAN - HALO), tiles(0, HALO)
    waits = []
    for place, (target, (inner, far)) in enumerate(zip(targets, sources)):
        pair = (
            copy_of(inner.at[..., inside, :], target.at[..., inside, :], sems.at[2 * place]),
            copy_of(far, target.at[..., outside, :], sems.at[2 * place + 1]),
        )
        for copy in pair:
            copy.start()
        waits.append(pair)

    def wait(place):
        for copy in waits[place]:
            copy.wait()

    return wait


def gradient(wait, e, east, same, other, values, spare, scale, lo):
    wait(0)
    for at in blocks_from(lo):
        for parity in range(2):
            term = get(e.at[parity], at, UNIT) * get(values.at[parity], at, UNIT)
            put(values.at[parity], at, scale * term)
    for place in (1, 2, 3):
        wait(place)
    diffuse(values, spare, east, same, other, inward(lo))


def middle_kernel(mine, other_core, e_in, e_far, east_in, east_far, same_in, same_far, other_in, other_far,
                  c_in, c_far, mine_out, other_out, c_hbm,
                  values, spare, e, east, same, other, c, c_new, sems, sem_out, *, scale):
    sources = ((e_in, e_far), (east_in, east_far), (same_in, same_far), (other_in, other_far), (c_in, c_far))
    wait = fetch(sources, (e, east, same, other, c), sems)
    spread(mine, other_core, values)
    gradient(wait, e, east, same, other, values, spare, scale, STEPS)
    wait(4)
    for at in blocks_from(2 * STEPS):
        for parity in range(2):
            new = get(c.at[parity], at, UNIT)
            new = new - step_size * (new + get(values.at[parity], at, UNIT))
            put(c_new.at[parity], at, new)
            put(values.at[parity], at, new)
    inside = tiles(HALO, SPAN - HALO)
    keep = copy_of(c_new.at[:, inside, :], c_hbm, sem_out)
    keep.start()
    diffuse(values, spare, east, same, other, inward(2 * STEPS))
    multiply(values, e, spare, blocks_from(3 * STEPS))
    lay_out(spare, mine_out, other_out)
    keep.wait()


def last_kernel(mine, other_core, e_in, e_far, east_in, east_far, same_in, same_far, other_in, other_far,
                c_in, out_hbm, values, spare, e, east, same, other, c, out, sems, sem_in, sem_out, *, scale):
    inside = tiles(HALO, SPAN - HALO)
    last = copy_of(c_in, c.at[:, inside, :], sem_in)
    sources = ((e_in, e_far), (east_in, east_far), (same_in, same_far), (other_in, other_far))
    wait = fetch(sources, (e, east, same, other), sems)
    last.start()
    spread(mine, other_core, values)
    gradient(wait, e, east, same, other, values, spare, scale, 3 * STEPS)
    last.wait()
    for at in blocks_from(HALO):
        for parity in range(2):
            new = get(c.at[parity], at, UNIT)
            put(values.at[parity], at, new - step_size * (new + get(values.at[parity], at, UNIT)))
    copies = []
    for member in range(2):
        for level in range(2):
            for parity in range(2):
                part = band_of(values.at[parity], 2 * member + level)
                out[member, level, pl.ds(parity, 128, stride=2), :] = part.T
            copy = copy_of(out.at[member, level], out_hbm.at[member, level], sem_out.at[2 * member + level])
            copy.start()
            copies.append(copy)
    for copy in copies:
        copy.wait()


def near_core(value):
    return pltpu.with_memory_space_constraint(value, pltpu.VMEM)


def call(kernel, outs, scratch, name, *args, far_in=(), far_out=()):
    here, far = pl.BlockSpec(memory_space=pltpu.VMEM), pl.BlockSpec(memory_space=pl.ANY)
    copied = not all(isinstance(part, tuple) for part in scratch)
    return pl.pallas_call(
        kernel,
        out_shape=[
            (jax.ShapeDtypeStruct if place in far_out else pltpu.VMEM)(shape, jnp.float32)
            for place, shape in enumerate(outs)
        ],
        in_specs=[far if place in far_in else here for place in range(len(args))],
        out_specs=[far if place in far_out and copied else here for place in range(len(outs))],
        scratch_shapes=[pltpu.VMEM(part, jnp.float32) if isinstance(part, tuple) else part for part in scratch],
        name=name,
    )(*args)


def swap_chips(parts):
    size = lax.axis_size("mem")
    groups = [list(range(core, size, 2)) for core in range(2)]
    return lax.all_to_all(parts, "mem", split_axis=0, concat_axis=0, tiled=True, axis_index_groups=groups)


def swap_cores(part):
    return lax.ppermute(part, "mem", [(i, i ^ 1) for i in range(lax.axis_size("mem"))])


def swap_bands(part, odd_up):
    bands = lax.axis_size("lon")
    return lax.ppermute(part, "lon", [(i, (i + 1 if (i % 2 == 1) == odd_up else i - 1) % bands) for i in range(bands)])


def body(ensemble, controls_start, kappa_east, kappa_north, innovation, obs_mask, gauge_index, gauge_precision):
    chips = lax.axis_size("mem") // 2
    scale = float(lax.axis_size("mem") * ensemble.shape[0]) ** (-0.5)
    field, one = (2, 8 * SIZE, 128), (8 * SIZE, 128)
    far_field, far_one, band = (2, 8 * HALO, 128), (8 * HALO, 128), (2, 8 * (SPAN - HALO), 128)
    parcel, parts, local, wide = (8 * SENT, 128), (chips, 3, 8, 128), (3, 8, 128), (4, 256, 128)
    sem = pltpu.SemaphoreType.DMA
    w, innov, first, second = call(
        edges_kernel, (innovation.shape, innovation.shape, parcel, parcel), (parcel, parcel, wide), "edges",
        controls_start, ensemble, kappa_east, kappa_north, innovation, obs_mask, gauge_index,
        gauge_precision.reshape(1, GAUGES),
    )
    near, far = near_core(swap_bands(first, True)), near_core(swap_bands(second, False))
    c, e, east, same, other, product, saved = call(
        inner_kernel, (field, field, field, one, one, field, (2, 8 * (2 * STEPS + 1), 128)), (field, field, field, wide),
        "inner", controls_start, ensemble, kappa_east, kappa_north, far_out=range(6),
    )
    w, innov, saved = near_core(w), near_core(innov), near_core(saved)
    mine, theirs, weight, innov, c_far, e_far, east_far, same_far, other_far = call(
        outer_kernel, (parts, parts, local, local, far_field, far_field, far_field, far_one, far_one),
        (field, field, field, field, field, field, field, one, one, sem((5,)), sem((5,))), "outer",
        near, far, w, innov, saved, e, east, same, other, product, far_in=range(5, 10), far_out=range(4, 9),
    )
    weight, innov = near_core(weight), near_core(innov)
    fixed = (e, e_far, east, east_far, same, same_far, other, other_far)

    def forced(mine, theirs, outs):
        kernel = lambda *refs: forcing_kernel(*refs, scale=scale)
        sums = near_core(swap_chips(mine + swap_cores(theirs)))
        forcing, *increment = call(kernel, outs, (), "forcing", sums, weight, innov)
        mine = swap_chips(forcing)
        return near_core(mine), near_core(swap_cores(mine)), *increment

    mine, theirs = forced(mine, theirs, (parts,))
    kernel = lambda *refs: middle_kernel(*refs, scale=scale)
    mine, theirs, c = call(
        kernel, (parts, parts, band), (field, field, field, field, one, one, field, field, sem((10,)), sem),
        "middle", mine, theirs, *fixed, c, c_far, far_in=range(2, 12), far_out=(2,),
    )
    mine, theirs, increment = forced(mine, theirs, (parts, innovation.shape))
    kernel = lambda *refs: last_kernel(*refs, scale=scale)
    (controls,) = call(
        kernel, (controls_start.shape,),
        (field, field, field, field, one, one, field, controls_start.shape, sem((8,)), sem, sem((4,))),
        "last", mine, theirs, *fixed, c, far_in=range(2, 11), far_out=(0,),
    )
    return controls, increment


def solution(mesh):
    in_specs = (
        P("mem", None, None, "lon"),
        P("mem", None, None, "lon"),
        P(None, None, "lon"),
        P(None, None, "lon"),
        P(None, "mem", "lon"),
        P(None, "mem", "lon"),
        P(None, "mem", "lon"),
        P(),
    )
    out_specs = (P("mem", None, None, "lon"), P(None, "mem", "lon"))
    return jax.shard_map(body, mesh=mesh, in_specs=in_specs, out_specs=out_specs, check_vma=False)
```
